256 devices in a mesh: leaf: 128 (over x, z, y), rhs: 2 (over core).
Axes of the slice: x: 4, y: 4, z: 8, core: 2. Of those that a mesh axis runs over, the one named last changes fastest.
Arguments:
- leaf_rhs: float32 [128, 512, 256], P('leaf', None, 'rhs'), may hold values from -6 to 6
- leaf_inv: bfloat16 [128, 512, 512], P('leaf', 'rhs'), as said below
- row_blocks: bfloat16 [128, 2496, 512], P('leaf'), may hold values from -0.046875 to 0.046875
- node_rhs: float32 [128, 704, 256], P('leaf', None, 'rhs'), may hold values from -6 to 6
- node_inv: bfloat16 [128, 1408, 512], P('leaf'), as said below
- sep_size: int32 [128], replicated, may hold values from 256 to 4096, as said below
Outputs:
- leaf_solution: float32 [128, 512, 256], P('leaf', None, 'rhs')
- node_solution: float32 [128, 704, 256], P('leaf', None, 'rhs')
The draws below stay inside these ranges and needn't reach their ends.
Inputs may be any that keep to these rules, and one draw needn't show every extreme that they name: For k >= 1, sep_size[k] lies between half of and all of the R_h rows of node k, h being its level; the root's (k = 1) is all of its rows. Entry 0 is 512 and is not read. `leaf_inv`: lower triangular. `node_inv`: each piece comes from a lower-triangular Inv_k: entry (a, b) of device d's level-h piece is zero where b < q_h(d) p_h + a.
All inputs are finite; a program needn't handle non-finite values.
Results may differ from the reference program's by a relative error of at most 0.0033.
Values may be sent and summed in bfloat16 or wider, within the bound.
No kernel may reach another device: no remote copies, remote signals or barrier semaphores. Data moves between devices by JAX's collectives and lax.ppermute only.
A program may use at most 64 MiB of HBM per device.

```python
import jax
import jax.numpy as jnp
from jax import lax

SEP = 512
RHS = 256
LEVELS = 7
ROOT_ROWS = 4096
SLAB_ROWS = 704
CPL_ROWS = 2496
N_LEAF = 128


def triangle_piece(key, salt, slab_rows, row_count, first_column):
    base = jax.random.fold_in(key, salt)
    piece_shape = (N_LEAF, slab_rows, row_count)
    below = jax.random.normal(jax.random.fold_in(base, 1), piece_shape, jnp.float32) / jnp.sqrt(row_count * 1.0)
    diagonal = jax.random.uniform(jax.random.fold_in(base, 2), (N_LEAF, slab_rows, 1), jnp.float32, 0.7, 1.3)
    column = first_column[:, None, None] + jnp.arange(slab_rows, dtype=jnp.int32)[None, :, None]
    target = jnp.arange(row_count, dtype=jnp.int32)[None, None, :]
    lower_part = jnp.where(target > column, below, jnp.zeros_like(below))
    return lower_part + jnp.where(target == column, diagonal, jnp.zeros_like(below))


def draw_leaf_inv(key, part):
    first_column = jnp.zeros((N_LEAF,), jnp.int32)
    piece = triangle_piece(key, 11, SEP, SEP, first_column)
    return jnp.swapaxes(piece, 1, 2).astype(jnp.bfloat16)


def draw_node_inv(key, part):
    device_ids = jnp.arange(N_LEAF, dtype=jnp.int32)
    pieces = []
    for height in range(1, LEVELS + 1):
        row_count = SEP * 2 ** ((height - 1) // 2)
        slab_rows = row_count >> height
        first_column = device_ids % 2 ** height * slab_rows
        piece = triangle_piece(key, 300 + height, slab_rows, row_count, first_column)
        pieces.append(piece.reshape(N_LEAF, slab_rows * row_count // SEP, SEP))
    return jnp.concatenate(pieces, axis=1).astype(jnp.bfloat16)


def draw_sep_size(key, part):
    node_ids = jnp.arange(N_LEAF, dtype=jnp.int32)
    depth = jnp.zeros((N_LEAF,), jnp.int32)
    for power in range(1, LEVELS + 1):
        depth = depth + (node_ids >= 2 ** power).astype(jnp.int32)
    height = LEVELS - depth
    full_rows = jnp.left_shift(jnp.full((N_LEAF,), SEP, jnp.int32), (height - 1) // 2).astype(jnp.int32)
    sizes = jax.random.randint(jax.random.fold_in(key, 201), (N_LEAF,), full_rows // 2, full_rows + 1).astype(jnp.int32)
    sizes = jnp.where(node_ids == 1, full_rows, sizes)
    sizes = jnp.where(node_ids == 0, SEP, sizes)
    return sizes.astype(jnp.int32)


def shard_levels(key, dims, cuts, least, top_value):
    def one(axis_at, blocks):
        draws = jax.random.uniform(jax.random.fold_in(jax.random.fold_in(key, 6), axis_at), (blocks,), jnp.float32, least / len(cuts), top_value / len(cuts))
        return jnp.repeat(jnp.exp(draws), dims[axis_at] // blocks).reshape((-1,) + (1,) * (len(dims) - axis_at - 1))

    gain = one(*cuts[0])
    for cut in cuts[1:]:
        gain = gain * one(*cut)
    return gain


def gaussian(stream_key, dims, width, most, split=(), kind=jnp.bfloat16):
    array = width * jax.random.normal(stream_key, dims, jnp.float32)
    if split:
        array = array * shard_levels(stream_key, dims, split, -0.22, 0.18)
    return jnp.clip(array, -most, most).astype(kind)


def setup_inputs(seed: int = 0) -> dict:
    key_of = jax.random.split(jax.random.key(seed), 7)
    leaf_rhs = gaussian(key_of[0], (N_LEAF, SEP, RHS), 1.0, 6.0, ((0, 128), (2, 2)), jnp.float32)
    leaf_inv = draw_leaf_inv(jax.random.fold_in(key_of[6], 71), 0)
    row_blocks = gaussian(key_of[2], (N_LEAF, CPL_ROWS, SEP), (4 * ROOT_ROWS) ** -0.5, 0.046875, ((0, 128),))
    node_rhs = gaussian(key_of[3], (N_LEAF, SLAB_ROWS, RHS), 1.0, 6.0, ((0, 128), (2, 2)), jnp.float32)
    node_inv = draw_node_inv(jax.random.fold_in(key_of[6], 71), 0)
    sep_size = draw_sep_size(jax.random.fold_in(key_of[6], 71), 0)
    return dict(leaf_rhs=leaf_rhs, leaf_inv=leaf_inv, row_blocks=row_blocks, node_rhs=node_rhs, node_inv=node_inv, sep_size=sep_size)


def level_rows(height):
    return SEP * 2 ** ((height - 1) // 2)


def reference(leaf_rhs, leaf_inv, row_blocks, node_rhs, node_inv, sep_size):
    def leaf_product(items):
        inverse, right_side = items
        return jnp.dot(inverse, right_side.astype(jnp.bfloat16), preferred_element_type=jnp.float32)

    leaf_solution = lax.map(leaf_product, (leaf_inv, leaf_rhs))
    rounded_list = [leaf_solution.astype(jnp.bfloat16)]
    device_ids = jnp.arange(N_LEAF, dtype=jnp.int32)
    slab_start = 0
    inverse_start = 0
    coupling_start = 0
    slab_pieces = []
    for height in range(1, LEVELS + 1):
        row_count = level_rows(height)
        slab_rows = row_count >> height
        node_count = N_LEAF >> height
        block_width = SEP + sum(level_rows(lower) for lower in range(1, height))
        coupling_count = slab_rows * block_width // SEP
        coupling = row_blocks[:, coupling_start:coupling_start + coupling_count].reshape(N_LEAF, slab_rows, block_width)

        def pending_one(device, coupling=coupling, height=height):
            block = lax.dynamic_index_in_dim(coupling, device, 0, keepdims=False)
            own_leaf = lax.dynamic_index_in_dim(rounded_list[0], device, 0, keepdims=False)
            total = jnp.dot(block[:, :SEP], own_leaf, preferred_element_type=jnp.float32)
            column_start = SEP
            for lower in range(1, height):
                lower_rows = level_rows(lower)
                below = lax.dynamic_index_in_dim(rounded_list[lower], device >> lower, 0, keepdims=False)
                total = total + jnp.dot(block[:, column_start:column_start + lower_rows], below, preferred_element_type=jnp.float32)
                column_start += lower_rows
            return total

        pending = lax.map(pending_one, device_ids)
        residual = node_rhs[:, slab_start:slab_start + slab_rows] - pending
        residual_rounded = residual.astype(jnp.bfloat16).reshape(node_count, row_count, RHS)
        inverse_count = slab_rows * row_count // SEP
        inverse_columns = node_inv[:, inverse_start:inverse_start + inverse_count].reshape(node_count, row_count, row_count)

        def node_product(items):
            columns, right_side = items
            return lax.dot_general(columns, right_side, (((0,), (0,)), ((), ())), preferred_element_type=jnp.float32)

        solved = lax.map(node_product, (inverse_columns, residual_rounded))
        counts = sep_size[node_count:2 * node_count]
        live_rows = jnp.arange(row_count, dtype=jnp.int32)[None, :] < counts[:, None]
        solved = jnp.where(live_rows[:, :, None], solved, jnp.zeros_like(solved))
        slab_pieces.append(solved.reshape(N_LEAF, slab_rows, RHS))
        rounded_list.append(solved.astype(jnp.bfloat16))
        slab_start += slab_rows
        inverse_start += inverse_count
        coupling_start += coupling_count
    node_solution = jnp.concatenate(slab_pieces, axis=1)
    return leaf_solution, node_solution
```

```python
import jax
import jax.numpy as jnp
from jax import lax
from jax.sharding import PartitionSpec as P

SEP = 512
LEAVES = 128
LEVELS = 7
BF16 = jnp.bfloat16
F32 = jnp.float32

Y_MASKS = (1, 2, 3)
X_MASKS = (32, 64, 96)


def level_rows(height):
    return SEP * 2 ** ((height - 1) // 2)


R = {h: level_rows(h) for h in range(1, LEVELS + 1)}
PR = {h: R[h] >> h for h in R}


def with_partner(x, mask):
    return lax.ppermute(x, "leaf", [(i, i ^ mask) for i in range(LEAVES)])


def along_z(x, step):
    pairs = []
    for i in range(LEAVES):
        z = i >> 2 & 7
        pairs.append((i, i & ~28 | ((z + step) & 7) << 2))
    return lax.ppermute(x, "leaf", pairs)


def swap_core(x):
    return lax.ppermute(x, "rhs", [(0, 1), (1, 0)])


def z_exchange(x):
    groups = [
        [y + 4 * z + 32 * xx for z in range(8)] for xx in range(4) for y in range(4)
    ]
    return lax.all_to_all(x, "leaf", 0, 0, axis_index_groups=groups, tiled=True)


def dot(a, b, ca=1, cb=0):
    return lax.dot_general(a, b, (((ca,), (cb,)), ((), ())), preferred_element_type=F32)


def split_sum(u):
    hi = lax.reduce_precision(u, 8, 7)
    return jnp.concatenate([hi.astype(BF16), (u - hi).astype(BF16)], 1)


def ring_gather(own):
    pieces = {0: own}
    up, down = own, own
    for step in (1, 2, 3):
        up = along_z(up, 1)
        down = along_z(down, -1)
        pieces[step] = up
        pieces[8 - step] = down
    pieces[4] = along_z(up, 1)
    rows = own.shape[0]
    z = lax.axis_index("leaf") >> 2 & 7
    ordered = [pieces[s] for s in range(7, -1, -1)]
    doubled = jnp.stack(ordered + ordered, 0)
    return lax.dynamic_slice_in_dim(doubled, 7 - z, 8, 0)


def local(leaf_rhs, leaf_inv, row_blocks, node_rhs, node_inv, sep_size):
    me = lax.axis_index("leaf")
    core = lax.axis_index("rhs")
    z = me >> 2 & 7

    o, e, c, width = {}, {}, {}, {}
    so = se = sc = 0
    for h in R:
        width[h] = SEP + sum(R[g] for g in range(1, h))
        o[h], e[h], c[h] = so, se, sc
        so += PR[h]
        se += PR[h] * R[h] // SEP
        sc += PR[h] * width[h] // SEP
    first = {1: 1}
    for h in range(2, LEVELS + 1):
        first[h] = first[h - 1] + R[h - 1] // SEP

    m_of = {
        h: row_blocks[0, c[h] : c[h] + PR[h] * width[h] // SEP].reshape(PR[h], width[h] // SEP, SEP)
        for h in R
    }

    def coupling(g, h):
        return m_of[g][:, first[h] : first[h] + R[h] // SEP].reshape(PR[g], R[h])

    def inverse(h):
        s = node_inv[0, e[h] : e[h] + PR[h] * R[h] // SEP].reshape(PR[h], R[h] // SEP, SEP)
        row = lax.broadcasted_iota(jnp.int32, (1, R[h] // SEP, SEP), 1) * SEP + lax.broadcasted_iota(
            jnp.int32, (1, R[h] // SEP, SEP), 2
        )
        live = row < sep_size[(LEAVES + me) >> h]
        return jnp.where(live, s, jnp.zeros_like(s))

    s1 = inverse(1).reshape(256, SEP)
    s2 = inverse(2).reshape(128, SEP)
    s12 = jnp.concatenate([s1, s2], 0)
    s12_1 = with_partner(s12, 1)
    inv1 = jnp.concatenate([s1, s12_1[:256]], 0)
    inv2 = jnp.concatenate([s2, s12_1[256:], with_partner(s2, 2), with_partner(s2, 3)], 0)

    def half_blocks(x, h):
        n = R[h] // SEP // 2
        mine = lax.dynamic_slice_in_dim(x, core * n, n, 1)
        return [mine[:, j] for j in range(n)]

    m_half = {}
    for h in (3, 4, 5, 6):
        parts = [half_blocks(m_of[g][:, first[h] : first[h] + R[h] // SEP], h) for g in range(h + 1, LEVELS + 1)]
        n = len(parts[0])
        m_half[h] = [jnp.concatenate([p[j] for p in parts], 0) for j in range(n)]
    m6 = jnp.concatenate(m_half[6], 0)
    m6x = with_partner(m6, 32)
    m_pack = jnp.concatenate(m_half[3] + m_half[4] + m_half[5] + [m6, m6x], 0)
    m_from = [m_pack] + [with_partner(m_pack, m) for m in Y_MASKS]

    def unpack(pack):
        out = {}
        out[3] = [pack[0:192]]
        out[4] = [pack[192:320]]
        out[5] = [pack[320:384], pack[384:448]]
        out[6] = [pack[448:480], pack[480:512]]
        out[7] = [pack[512:544], pack[544:576]]
        return out

    m_rows = [unpack(p) for p in m_from]

    s_half = {h: half_blocks(inverse(h), h) for h in (3, 4, 5, 6)}
    s34 = jnp.concatenate(s_half[3] + s_half[4], 0)
    s34_1 = with_partner(s34, 4)
    inv_half = {
        3: [jnp.concatenate([s_half[3][0], s34_1[:128]], 0)],
        4: [
            jnp.concatenate(
                [s_half[4][0], s34_1[128:], with_partner(s_half[4][0], 8), with_partner(s_half[4][0], 12)], 0
            )
        ],
    }
    s56 = jnp.concatenate(s_half[5] + s_half[6], 0)
    ring = ring_gather(s56)
    inv_half[5] = [ring[:, 0:64].reshape(512, SEP), ring[:, 64:128].reshape(512, SEP)]
    inv_half[6] = [ring[:, 128:160].reshape(256, SEP), ring[:, 160:192].reshape(256, SEP)]

    def select_rows(h, masks):
        n = R[h] // SEP // 2
        start = jnp.stack([((me ^ m) & ((1 << h) - 1)) * PR[h] for m in masks])
        shape = (len(masks), PR[h], n * SEP)
        row = start[:, None, None] + lax.broadcasted_iota(jnp.int32, shape, 1)
        col = core * (n * SEP) + lax.broadcasted_iota(jnp.int32, shape, 2)
        hot = (row == col).astype(BF16).reshape(len(masks) * PR[h], n * SEP)
        return [hot[:, j * SEP : (j + 1) * SEP] for j in range(n)]

    def product(h, masks, m_list):
        sel = select_rows(h, masks)
        u = None
        for j in range(len(sel)):
            left = jnp.concatenate([sel[j]] + [m[j] for m in m_list], 0)
            term = dot(left, inv_half[h][j], 1, 1)
            u = term if u is None else u + term
        u = u + swap_core(u)
        return u

    y_all = (0,) + Y_MASKS
    v_self, v_up = {}, {}
    for h in (3, 4, 5):
        u = product(h, y_all, [m_rows[k][h] for k in range(4)])
        v_self[h] = u[: 4 * PR[h]].astype(BF16)
        above = u[4 * PR[h] :].reshape(4, -1, u.shape[1])
        at = 0
        for g in range(h + 1, LEVELS + 1):
            v_up[g, h] = split_sum(above[:, at : at + PR[g]].reshape(4 * PR[g], -1))
            at += PR[g]
    masks6 = y_all + tuple(32 + m for m in y_all)
    u = product(6, masks6, [m_rows[k][6] for k in range(4)] + [m_rows[k][7] for k in range(4)])
    v_self[6] = u[:256].astype(BF16)
    v_up[7, 6] = split_sum(u[256:])

    linv = lax.all_gather(leaf_inv, "rhs", axis=1, tiled=True)[0]
    x0 = dot(linv, leaf_rhs[0].astype(BF16))
    x0b = x0.astype(BF16)
    b = {h: node_rhs[0, o[h] : o[h] + PR[h]] for h in R}
    r1 = (b[1] - dot(m_of[1][:, 0], x0b)).astype(BF16)
    m0 = jnp.concatenate([m_of[h][:, 0] for h in range(2, LEVELS + 1)], 0)
    g_rest = node_rhs[0, o[2] :] - dot(m0, x0b)

    outs = {}
    r1_all = jnp.concatenate([r1, with_partner(r1, 1)], 0)
    x1 = dot(inv1, r1_all, 0, 0)
    outs[1] = lax.dynamic_slice_in_dim(x1, (me & 1) * 256, 256, 0)
    x1b = x1.astype(BF16)
    m1 = jnp.concatenate([coupling(g, 1) for g in range(2, LEVELS + 1)], 0)
    g_rest = g_rest - dot(m1, x1b)
    r2 = g_rest[:128].astype(BF16)
    r2_all = jnp.concatenate([r2] + [with_partner(r2, m) for m in Y_MASKS], 0)
    x2 = dot(inv2, r2_all, 0, 0)
    outs[2] = lax.dynamic_slice_in_dim(x2, (me & 3) * 128, 128, 0)
    x2b = x2.astype(BF16)
    m2 = jnp.concatenate([coupling(g, 2) for g in range(3, LEVELS + 1)], 0)
    g_rest = g_rest[128:] - dot(m2, x2b)
    g = {h: g_rest[o[h] - o[3] : o[h] - o[3] + PR[h]] for h in range(3, LEVELS + 1)}

    def gather_z(h, r):
        if h == 3:
            return jnp.concatenate([r, with_partner(r, 4)], 0)
        if h == 4:
            return jnp.concatenate([r, with_partner(r, 4), with_partner(r, 8), with_partner(r, 12)], 0)
        return z_exchange(jnp.broadcast_to(r[None], (8,) + r.shape)).reshape(8 * PR[h], 128)

    def scatter_y(p):
        total = p[0]
        for k, m in enumerate(Y_MASKS):
            total = total + with_partner(p[k + 1], m)
        return total

    up = {}
    own = {}
    for h in (3, 4, 5, 6):
        r = g[h].astype(BF16)
        if h == 5:
            s7 = node_inv[0, e[7] : e[7] + 256].reshape(32, 4, 2, 4, 128)
            s7 = s7.transpose(2, 3, 1, 0, 4).reshape(8, 4, 32, 128)
            s7 = lax.dynamic_slice_in_dim(s7, core * 16, 16, 2).reshape(8, 64, 128)
            both = jnp.concatenate([jnp.broadcast_to(r[None], (8, 64, 128)), s7], 1)
            got = z_exchange(both)
            r_all = got[:, :64].reshape(512, 128)
            s7_mine = got[:, 64:]
        else:
            r_all = gather_z(h, r)
        r_two = jnp.concatenate([r_all, r_all], 0)
        own[h] = dot(v_self[h], r_all)
        for t in range(h + 1, LEVELS + 1):
            term = dot(v_up[t, h], r_two)
            if h < 6:
                term = term.reshape(4, PR[t], 128)
                up[t] = term if t not in up else up[t] + term
        if h < 6:
            g[h + 1] = g[h + 1] - scatter_y(up[h + 1])
        else:
            term = term.reshape(2, 4, 32, 128)
            term = jnp.concatenate([term[0] + up[7], term[1]], 1)
            part = scatter_y(term)
            g[7] = g[7] - (part[:32] + with_partner(part[32:], 32))

    s7_other = swap_core(s7_mine)
    low = jnp.where(core == 0, s7_mine, s7_other).reshape(8, 4, 16, 128)
    high = jnp.where(core == 0, s7_other, s7_mine).reshape(8, 4, 16, 128)
    s7_all = jnp.concatenate([low, high], 2)
    s7_all = s7_all.transpose(1, 0, 2, 3).reshape(4, 256, 128)
    r7 = gather_z(7, g[7].astype(BF16))
    p7 = jnp.stack([dot(s7_all[k], r7, 0, 0) for k in range(4)], 0).reshape(4, 4, 32, 128)
    yy = me & 3
    xx = me >> 5
    p7 = jnp.where((xx & 1) == 0, p7, jnp.stack([p7[1], p7[0], p7[3], p7[2]], 0))
    p7 = jnp.where((xx & 2) == 0, p7, jnp.stack([p7[2], p7[3], p7[0], p7[1]], 0))
    p7 = jnp.where((yy & 1) == 0, p7, jnp.stack([p7[:, 1], p7[:, 0], p7[:, 3], p7[:, 2]], 1))
    p7 = jnp.where((yy & 2) == 0, p7, jnp.stack([p7[:, 2], p7[:, 3], p7[:, 0], p7[:, 1]], 1))

    lower = jnp.concatenate([own[h].reshape(4, PR[h], 128) for h in (3, 4, 5)], 1)
    lower = scatter_y(lower)
    outs[3], outs[4], outs[5] = lower[:128], lower[128:192], lower[192:256]

    last = p7.transpose(1, 0, 2, 3).reshape(4, 128, 128)
    six = own[6].reshape(2, 4, 32, 128).transpose(1, 0, 2, 3).reshape(4, 64, 128)
    part = scatter_y(jnp.concatenate([last, six], 1))
    near = with_partner(jnp.concatenate([part[32:64], part[160:192]], 0), 32)
    outs[7] = part[:32] + near[:32] + with_partner(part[64:96], 64) + with_partner(part[96:128], 96)
    outs[6] = part[128:160] + near[32:]
    live7 = me * 32 + lax.broadcasted_iota(jnp.int32, (32, 1), 0) < sep_size[1]
    outs[7] = jnp.where(live7, outs[7], jnp.zeros_like(outs[7]))
    node_solved = jnp.concatenate([outs[h] for h in R], 0)
    return x0[None], node_solved[None]


def solution(mesh):
    in_specs = (
        P("leaf", None, "rhs"),
        P("leaf", "rhs", None),
        P("leaf", None, None),
        P("leaf", None, "rhs"),
        P("leaf", None, None),
        P(),
    )
    out_specs = (P("leaf", None, "rhs"), P("leaf", None, "rhs"))
    return jax.shard_map(local, mesh=mesh, in_specs=in_specs, out_specs=out_specs, check_vma=False)
```

```python
import functools

import jax
import jax.numpy as jnp
from jax import lax
from jax.experimental import pallas as pl
from jax.experimental.pallas import tpu as pltpu
from jax.sharding import PartitionSpec as P

SEP = 512
LEAVES = 128
LEVELS = 7
BF16 = jnp.bfloat16
F32 = jnp.float32

Y_MASKS = (1, 2, 3)


def level_rows(height):
    return SEP * 2 ** ((height - 1) // 2)


R = {h: level_rows(h) for h in range(1, LEVELS + 1)}
PR = {h: R[h] >> h for h in R}
WIDTH = {h: SEP + sum(R[g] for g in range(1, h)) for h in R}
OFF_O, OFF_E, OFF_C = {}, {}, {}
_o = _e = _c = 0
for _h in R:
    OFF_O[_h], OFF_E[_h], OFF_C[_h] = _o, _e, _c
    _o += PR[_h]
    _e += PR[_h] * R[_h] // SEP
    _c += PR[_h] * WIDTH[_h] // SEP
FIRST = {1: 1}
for _h in range(2, LEVELS + 1):
    FIRST[_h] = FIRST[_h - 1] + R[_h - 1] // SEP
ABOVE = {h: sum(PR[g] for g in range(h + 1, LEVELS + 1)) for h in range(3, 7)}


def with_partner(x, mask):
    return lax.ppermute(x, "leaf", [(i, i ^ mask) for i in range(LEAVES)])


def along_z(x, step):
    pairs = []
    for i in range(LEAVES):
        z = i >> 2 & 7
        pairs.append((i, i & ~28 | ((z + step) & 7) << 2))
    return lax.ppermute(x, "leaf", pairs)


def swap_core(x):
    return lax.ppermute(x, "rhs", [(0, 1), (1, 0)])


def z_exchange(x):
    groups = [[y + 4 * z + 32 * xx for z in range(8)] for xx in range(4) for y in range(4)]
    return lax.all_to_all(x, "leaf", 0, 0, axis_index_groups=groups, tiled=True)


def dot(a, b, ca=1, cb=0):
    return lax.dot_general(a, b, (((ca,), (cb,)), ((), ())), preferred_element_type=F32)


def one_hot(match):
    return jnp.where(match, 1.0, 0.0).astype(BF16)


def iota(shape, axis):
    return lax.broadcasted_iota(jnp.int32, shape, axis)


def call(kernel, out_shapes, args, scratch=(), flops=10**9):
    moved = sum(a.size * a.dtype.itemsize for a in args) + sum(
        s.size * s.dtype.itemsize for s in out_shapes
    )
    specs = [pl.BlockSpec(memory_space=pltpu.SMEM)] + [pl.BlockSpec(memory_space=pltpu.VMEM)] * (len(args) - 1)
    return pl.pallas_call(
        kernel,
        out_shape=out_shapes,
        in_specs=specs,
        out_specs=[pl.BlockSpec(memory_space=pltpu.VMEM)] * len(out_shapes),
        scratch_shapes=list(scratch),
        compiler_params=pltpu.CompilerParams(vmem_limit_bytes=40 * 2**20),
        cost_estimate=pl.CostEstimate(flops=flops, bytes_accessed=moved, transcendentals=0),
    )(*args)


def after(x, *values):
    return lax.optimization_barrier((x, *values))[0]


def struct(shape, dtype):
    return jax.ShapeDtypeStruct(shape, dtype)


def regroup(x, rows, width):
    n = rows * width
    shift = rows.bit_length() - 1
    t = iota((n, n), 0)
    source = (t & (rows - 1)) * width + lax.shift_right_logical(t, shift)
    return dot(one_hot(source == iota((n, n), 1)), x).astype(BF16)


def pack_kernel(scal, rb, ni, m0, m1, m2, mp3, mpr, s34, s56, s7, held):
    core = scal[1]
    for g in range(2, LEVELS + 1):
        p, w = PR[g], WIDTH[g] // SEP
        n = p * w
        held[0:n, :] = regroup(rb[OFF_C[g] : OFF_C[g] + n, :], p, w)

        def rows(j):
            return held[pl.ds(pl.multiple_of(j * p, 32), p), :]

        m0[OFF_O[g] - 256 : OFF_O[g] - 256 + p, :] = held[0:p, :]
        m1[OFF_O[g] - 256 : OFF_O[g] - 256 + p, :] = held[p : 2 * p, :]
        if g >= 3:
            m2[OFF_O[g] - 384 : OFF_O[g] - 384 + p, :] = held[2 * p : 3 * p, :]
        if g >= 4:
            at = OFF_O[g] - OFF_O[4]
            mp3[at : at + p, :] = rows(FIRST[3] + core)
        if g >= 5:
            at = OFF_O[g] - OFF_O[5]
            mpr[at : at + p, :] = rows(FIRST[4] + core)
        if g >= 6:
            at = OFF_O[g] - OFF_O[6]
            for j in range(2):
                mpr[128 + 64 * j + at : 128 + 64 * j + at + p, :] = rows(FIRST[5] + 2 * core + j)
        if g == 7:
            for j in range(2):
                mpr[256 + 32 * j : 288 + 32 * j, :] = rows(FIRST[6] + 2 * core + j)
    for h in range(3, LEVELS + 1):
        p, w = PR[h], R[h] // SEP
        n = p * w
        held[0:n, :] = regroup(ni[OFF_E[h] : OFF_E[h] + n, :], p, w)
        if h == 7:
            for zz in range(8):
                for xx in range(4):
                    block = 2 * xx + (zz >> 2)
                    start = pl.multiple_of(block * 32 + core * 16, 16)
                    s7[zz, xx * 16 : xx * 16 + 16, :] = held[
                        pl.ds(start, 16), (zz & 3) * 128 : (zz & 3) * 128 + 128
                    ]
            continue
        target, at = {3: (s34, 0), 4: (s34, 128), 5: (s56, 0), 6: (s56, 128)}[h]
        for j in range(w // 2):
            block = core * (w // 2) + j
            x = held[pl.ds(pl.multiple_of(block * p, 32), p), :]
            live = block * SEP + iota((p, SEP), 1) < scal[1 + h]
            target[at + j * p : at + j * p + p, :] = jnp.where(live, x, jnp.zeros_like(x))


def products(h, scal, left_rows, inv, u):
    me, core = scal[0], scal[1]
    p, above = PR[h], ABOVE[h]
    n = R[h] // SEP // 2
    for k in range(4):
        total = None
        top = None
        for j in range(n):
            start = ((me ^ k) & ((1 << h) - 1)) * p - (core * n + j) * SEP
            sel = one_hot(iota((p, SEP), 1) == start + iota((p, SEP), 0))
            right = inv(j)
            a = dot(sel, right, 1, 1)
            b = dot(left_rows(k, j), right, 1, 1)
            top = a if top is None else top + a
            total = b if total is None else total + b
        u[k * p : k * p + p, :] = top
        u[4 * p + k * above : 4 * p + (k + 1) * above, :] = total


def product3_kernel(scal, l0, l1, l2, l3, s, sp, u, inv):
    inv[0:128, :] = s[0:128, :]
    inv[128:256, :] = sp[0:128, :]
    lefts = (l0, l1, l2, l3)
    products(3, scal, lambda k, j: lefts[k][...], lambda j: inv[...], u)


def product4_kernel(scal, l0, l1, l2, l3, s, s1, s2, s3, u, inv):
    inv[0:64, :] = s[128:192, :]
    inv[64:128, :] = s1[128:192, :]
    inv[128:192, :] = s2[...]
    inv[192:256, :] = s3[...]
    lefts = (l0, l1, l2, l3)
    products(4, scal, lambda k, j: lefts[k][0:128, :], lambda j: inv[...], u)


def product5_kernel(scal, l0, l1, l2, l3, r0, r1, r2, r3, r4, r5, r6, r7, u, inv6, inv):
    z = lax.shift_right_logical(scal[0], 2) & 7
    for s, piece in enumerate((r0, r1, r2, r3, r4, r5, r6, r7)):
        at = (z - s) & 7
        for j in range(2):
            inv[j, pl.ds(pl.multiple_of(at * 64, 64), 64), :] = piece[64 * j : 64 * j + 64, :]
            inv6[j, pl.ds(pl.multiple_of(at * 32, 32), 32), :] = piece[128 + 32 * j : 160 + 32 * j, :]
    lefts = (l0, l1, l2, l3)
    products(5, scal, lambda k, j: lefts[k][128 + 64 * j : 192 + 64 * j, :], lambda j: inv[j], u)


def product6_kernel(scal, l0, l1, l2, l3, mine, other, u, inv):
    for j in range(2):
        for zz in range(8):
            inv[j, 64 * zz : 64 * zz + 32, :] = mine[j, 32 * zz : 32 * zz + 32, :]
            inv[j, 64 * zz + 32 : 64 * zz + 64, :] = other[j, 32 * zz : 32 * zz + 32, :]
    lefts = (l0, l1, l2, l3)
    products(6, scal, lambda k, j: lefts[k][256 + 32 * j : 288 + 32 * j, :], lambda j: inv[j], u)


def finish_kernel(h, scal, ua, ub, own, *ups):
    p, above = PR[h], ABOVE[h]
    cols = ua.shape[1]
    own[...] = (ua[0 : 4 * p, :] + ub[0 : 4 * p, :]).astype(BF16)
    at = 0
    for t, up in zip(range(h + 1, LEVELS + 1), ups):
        for k in range(4):
            start = 4 * p + k * above + at
            x = ua[start : start + PR[t], :] + ub[start : start + PR[t], :]
            hi = x.astype(BF16)
            up[k * PR[t] : (k + 1) * PR[t], 0:cols] = hi
            up[k * PR[t] : (k + 1) * PR[t], cols : 2 * cols] = (x - hi.astype(F32)).astype(BF16)
        at += PR[t]


def local(leaf_rhs, leaf_inv, row_blocks, node_rhs, node_inv, sep_size):
    me = lax.axis_index("leaf")
    core = lax.axis_index("rhs")
    sizes = [sep_size[(LEAVES + me) >> h] for h in R]
    scal = jnp.stack([me, core, sizes[0], sizes[1]] + sizes[2:] + [me] * 7).astype(jnp.int32)

    row12 = iota((384, 1), 0)
    live12 = iota((384, SEP), 1) < jnp.where(row12 < 256, sizes[0], sizes[1])
    s12 = node_inv[0, :384]
    s12 = jnp.where(live12, s12, jnp.zeros_like(s12))
    s2 = s12[256:]
    s12_1 = with_partner(s12, 1)
    inv1 = jnp.concatenate([s12[:256], s12_1[:256]], 0)
    inv2 = jnp.concatenate([s2, s12_1[256:], with_partner(s2, 2), with_partner(s2, 3)], 0)

    m0, m1, m2, mp3, mpr, s34, s56, s7 = call(
        pack_kernel,
        [
            struct((448, SEP), BF16),
            struct((448, SEP), BF16),
            struct((320, SEP), BF16),
            struct((192, SEP), BF16),
            struct((320, SEP), BF16),
            struct((192, SEP), BF16),
            struct((192, SEP), BF16),
            struct((8, 64, 128), BF16),
        ],
        (scal, row_blocks[0], node_inv[0]),
        [pltpu.VMEM((480, SEP), BF16)],
    )
    mp3_all = [mp3] + [with_partner(mp3, m) for m in Y_MASKS]
    s34_1 = with_partner(s34, 4)

    v_own, v_up = {}, {}

    def finish(h, u, gate):
        cols = u[0].shape[1]
        shapes = [struct((4 * PR[h], cols), BF16)]
        shapes += [struct((4 * PR[t], 2 * cols), BF16) for t in range(h + 1, LEVELS + 1)]
        got = call(functools.partial(finish_kernel, h), shapes, (after(scal, gate), u[0], u[1]), flops=10**6)
        v_own[h] = got[0]
        for t in range(h + 1, LEVELS + 1):
            v_up[t, h] = got[t - h]

    def u_shape(h, cols):
        return struct((4 * PR[h] + 4 * ABOVE[h], cols), F32)

    linv = lax.all_gather(leaf_inv, "rhs", axis=1, tiled=True)[0]
    x0 = dot(linv, leaf_rhs[0].astype(BF16))
    x0b = x0.astype(BF16)
    r1 = (node_rhs[0, :256] - dot(row_blocks[0, :256], x0b)).astype(BF16)
    g_rest = node_rhs[0, 256:] - dot(m0, x0b)

    outs = {}
    r1_all = jnp.concatenate([r1, with_partner(r1, 1)], 0)
    mpr, s56, s4 = after(mpr, r1), after(s56, r1), after(s34[128:], r1)
    mpr_all = [mpr] + [with_partner(mpr, m) for m in Y_MASKS]
    s4_2, s4_3 = with_partner(s4, 8), with_partner(s4, 12)
    ring = {0: s56}
    up_piece, down_piece = s56, s56
    for step in (1, 2, 3):
        up_piece = along_z(up_piece, 1)
        down_piece = along_z(down_piece, -1)
        ring[step] = up_piece
        ring[8 - step] = down_piece
    ring[4] = along_z(up_piece, 1)
    x1 = dot(inv1, r1_all, 0, 0)
    outs[1] = lax.dynamic_slice_in_dim(x1, (me & 1) * 256, 256, 0)
    g_rest = g_rest - dot(m1, x1.astype(BF16))
    r2 = g_rest[:128].astype(BF16)
    r2_all = jnp.concatenate([r2] + [with_partner(r2, m) for m in Y_MASKS], 0)
    (u3,) = call(
        product3_kernel,
        [u_shape(3, 256)],
        (after(scal, r2), *mp3_all, s34, s34_1),
        [pltpu.VMEM((256, SEP), BF16)],
    )
    u3 = (u3, swap_core(u3))
    x2 = dot(inv2, r2_all, 0, 0)
    outs[2] = lax.dynamic_slice_in_dim(x2, (me & 3) * 128, 128, 0)
    g_rest = g_rest[128:] - dot(m2, x2.astype(BF16))
    g = {h: g_rest[OFF_O[h] - 384 : OFF_O[h] - 384 + PR[h]] for h in range(3, LEVELS + 1)}

    def gather_z(r):
        return z_exchange(jnp.broadcast_to(r[None], (8,) + r.shape)).reshape(8 * r.shape[0], 128)

    def scatter_y(p):
        total = p[0]
        for k, m in enumerate(Y_MASKS):
            total = total + with_partner(p[k + 1], m)
        return total

    up = {}
    own = {}
    for h in (3, 4, 5, 6):
        r = g[h].astype(BF16)
        if h == 3:
            r_all = jnp.concatenate([r, with_partner(r, 4)], 0)
            finish(3, u3, r)
            (u4,) = call(
                product4_kernel,
                [u_shape(4, 256)],
                (after(scal, r), *mpr_all, s34, s34_1, s4_2, s4_3),
                [pltpu.VMEM((256, SEP), BF16)],
            )
            u4 = (u4, swap_core(u4))
        elif h == 4:
            r_all = jnp.concatenate([r, with_partner(r, 4), with_partner(r, 8), with_partner(r, 12)], 0)
            u5, inv6 = call(
                product5_kernel,
                [u_shape(5, 512), struct((2, 256, SEP), BF16)],
                (after(scal, r), *mpr_all, *[ring[s] for s in range(8)]),
                [pltpu.VMEM((2, 512, SEP), BF16)],
            )
            u5 = (u5, swap_core(u5))
            inv6x = with_partner(inv6, 32)
        elif h == 5:
            got = z_exchange(jnp.concatenate([jnp.broadcast_to(r[None], (8, 64, 128)), s7], 1))
            r_all = got[:, :64].reshape(512, 128)
            s7_mine = got[:, 64:]
            (u6,) = call(
                product6_kernel,
                [u_shape(6, 512)],
                (after(scal, r), *mpr_all, inv6, inv6x),
                [pltpu.VMEM((2, 512, SEP), BF16)],
            )
            u6 = (u6, swap_core(u6))
        else:
            r_all = gather_z(jnp.concatenate([r, with_partner(r, 32)], 0))
        r_two = jnp.concatenate([r_all, r_all], 0)
        for t in range(h + 1, LEVELS + 1):
            term = dot(v_up[t, h], r_two).reshape(4, PR[t], 128)
            up[t] = term if t not in up else up[t] + term
        if h == 3:
            finish(4, u4, up[4])
        elif h == 4:
            finish(5, u5, up[5])
        elif h == 5:
            finish(6, u6, up[6])
        g[h + 1] = g[h + 1] - scatter_y(up[h + 1])
        own[h] = dot(v_own[h], r_all).reshape(4, PR[h], 128)

    s7_other = swap_core(s7_mine)
    low = jnp.where(core == 0, s7_mine, s7_other).reshape(8, 4, 16, 128)
    high = jnp.where(core == 0, s7_other, s7_mine).reshape(8, 4, 16, 128)
    s7_all = jnp.concatenate([low, high], 2)
    s7_all = s7_all.transpose(1, 0, 2, 3).reshape(4, 256, 128)
    r7 = g[7].astype(BF16)
    lower, r7 = lax.optimization_barrier((jnp.concatenate([own[h] for h in (3, 4, 5, 6)], 1), r7))
    lower = scatter_y(lower)
    r7_all = gather_z(r7)
    p7 = jnp.stack([dot(s7_all[k], r7_all, 0, 0) for k in range(4)], 0).reshape(4, 4, 32, 128)
    yy = me & 3
    xx = me >> 5
    p7 = jnp.where((xx & 1) == 0, p7, jnp.stack([p7[1], p7[0], p7[3], p7[2]], 0))
    p7 = jnp.where((xx & 2) == 0, p7, jnp.stack([p7[2], p7[3], p7[0], p7[1]], 0))
    p7 = jnp.where((yy & 1) == 0, p7, jnp.stack([p7[:, 1], p7[:, 0], p7[:, 3], p7[:, 2]], 1))
    p7 = jnp.where((yy & 2) == 0, p7, jnp.stack([p7[:, 2], p7[:, 3], p7[:, 0], p7[:, 1]], 1))
    last = p7.transpose(1, 0, 2, 3).reshape(4, 128, 128)
    last, lower = lax.optimization_barrier((last, lower))
    outs[3], outs[4], outs[5], outs[6] = lower[:128], lower[128:192], lower[192:256], lower[256:]
    part = scatter_y(last)
    outs[7] = (
        part[:32]
        + with_partner(part[32:64], 32)
        + with_partner(part[64:96], 64)
        + with_partner(part[96:128], 96)
    )
    live7 = me * 32 + iota((32, 1), 0) < sep_size[1]
    outs[7] = jnp.where(live7, outs[7], jnp.zeros_like(outs[7]))
    node_solved = jnp.concatenate([outs[h] for h in R], 0)
    return x0[None], node_solved[None]


def solution(mesh):
    in_specs = (
        P("leaf", None, "rhs"),
        P("leaf", "rhs", None),
        P("leaf", None, None),
        P("leaf", None, "rhs"),
        P("leaf", None, None),
        P(),
    )
    out_specs = (P("leaf", None, "rhs"), P("leaf", None, "rhs"))
    return jax.shard_map(local, mesh=mesh, in_specs=in_specs, out_specs=out_specs, check_vma=False)
```

```python
import functools

import jax
import jax.numpy as jnp
from jax import lax
from jax.experimental import pallas as pl
from jax.experimental.pallas import tpu as pltpu
from jax.sharding import PartitionSpec as P


SEP = 512
LEAVES = 128
LEVELS = 7
BF16 = jnp.bfloat16
F32 = jnp.float32

Y_MASKS = (1, 2, 3)
Z_MASKS = (4, 8, 12)
X_MASKS = (32, 64, 96)


def level_rows(height):
    return SEP * 2 ** ((height - 1) // 2)


R = {h: level_rows(h) for h in range(1, LEVELS + 1)}
PR = {h: R[h] >> h for h in R}
WIDTH = {h: SEP + sum(R[g] for g in range(1, h)) for h in R}
OFF_O, OFF_E, OFF_C = {}, {}, {}
_o = _e = _c = 0
for _h in R:
    OFF_O[_h], OFF_E[_h], OFF_C[_h] = _o, _e, _c
    _o += PR[_h]
    _e += PR[_h] * R[_h] // SEP
    _c += PR[_h] * WIDTH[_h] // SEP
FIRST = {1: 1}
for _h in range(2, LEVELS + 1):
    FIRST[_h] = FIRST[_h - 1] + R[_h - 1] // SEP
ABOVE = {h: sum(PR[g] for g in range(h + 1, LEVELS + 1)) for h in range(3, 7)}


def with_partner(x, mask):
    return lax.ppermute(x, "leaf", [(i, i ^ mask) for i in range(LEAVES)])


def swap_core(x):
    return lax.ppermute(x, "rhs", [(0, 1), (1, 0)])


def dot(a, b, ca=1, cb=0):
    return lax.dot_general(a, b, (((ca,), (cb,)), ((), ())), preferred_element_type=F32)


def one_hot(match):
    return jnp.where(match, 1.0, 0.0).astype(BF16)


def iota(shape, axis):
    return lax.broadcasted_iota(jnp.int32, shape, axis)


def position():
    return lax.axis_index("leaf"), lax.axis_index("rhs")


def call(kernel, out_shapes, args, scratch=(), flops=10**8, smem=0, specs=None):
    moved = sum(a.size * a.dtype.itemsize for a in args) + sum(
        s.size * s.dtype.itemsize for s in out_shapes
    )
    if specs is None:
        specs = [pl.BlockSpec(memory_space=pltpu.SMEM)] * smem
        specs += [pl.BlockSpec(memory_space=pltpu.VMEM)] * (len(args) - smem)
    return pl.pallas_call(
        kernel,
        out_shape=out_shapes,
        in_specs=specs,
        out_specs=[pl.BlockSpec(memory_space=pltpu.VMEM)] * len(out_shapes),
        scratch_shapes=list(scratch),
        compiler_params=pltpu.CompilerParams(vmem_limit_bytes=40 * 2**20),
        cost_estimate=pl.CostEstimate(flops=flops, bytes_accessed=moved, transcendentals=0),
    )(*args)


def after(x, *values):
    return lax.optimization_barrier((x, *values))[0]


def struct(shape, dtype):
    return jax.ShapeDtypeStruct(shape, dtype)


def regroup(x, rows, width):
    n = rows * width
    shift = rows.bit_length() - 1
    t = iota((n, n), 0)
    source = (t & (rows - 1)) * width + lax.shift_right_logical(t, shift)
    return dot(one_hot(source == iota((n, n), 1)), x).astype(BF16)


def live_size(sizes, h):
    return sizes[lax.shift_right_logical(LEAVES + position()[0], h)]


def first_kernel(sizes, ni, s12):
    for h, at, n in ((1, 0, 256), (2, 256, 128)):
        x = ni[0, at : at + n, :]
        live = iota((n, SEP), 1) < live_size(sizes, h)
        s12[at : at + n, :] = jnp.where(live, x, jnp.zeros_like(x))


def pack_kernel(sizes, rb, ni, m0, m1, m2, mp34, mp56, z0, z1, z2, z3, held):
    me, core = position()
    z = lax.shift_right_logical(me, 2) & 7
    for g in range(2, LEVELS + 1):
        p, w = PR[g], WIDTH[g] // SEP
        n = p * w
        held[0:n, :] = regroup(rb[OFF_C[g] : OFF_C[g] + n, :], p, w)

        def rows(j):
            return held[pl.ds(pl.multiple_of(j * p, 32), p), :]

        m0[OFF_O[g] - 256 : OFF_O[g] - 256 + p, :] = held[0:p, :]
        m1[OFF_O[g] - 256 : OFF_O[g] - 256 + p, :] = held[p : 2 * p, :]
        if g >= 3:
            m2[OFF_O[g] - 384 : OFF_O[g] - 384 + p, :] = held[2 * p : 3 * p, :]
        if g >= 4:
            at = OFF_O[g] - OFF_O[4]
            mp34[at : at + p, :] = rows(FIRST[3] + core)
        if g >= 5:
            at = 192 + OFF_O[g] - OFF_O[5]
            mp34[at : at + p, :] = rows(FIRST[4] + core)
        if g >= 6:
            at = OFF_O[g] - OFF_O[6]
            for j in range(2):
                mp56[64 * j + at : 64 * j + at + p, :] = rows(FIRST[5] + 2 * core + j)
        if g == 7:
            for j in range(2):
                mp56[128 + 32 * j : 160 + 32 * j, :] = rows(FIRST[6] + 2 * core + j)
    for h in range(3, LEVELS + 1):
        p, w = PR[h], R[h] // SEP
        n = p * w
        held[0:n, :] = regroup(ni[OFF_E[h] : OFF_E[h] + n, :], p, w)
        if h == 7:
            for k, target in enumerate((z0, z1, z2, z3)):
                for half in range(2):
                    to = z ^ k ^ (4 * half)
                    lane = pl.multiple_of((to & 3) * 128, 128)
                    for xx in range(4):
                        start = (2 * xx + lax.shift_right_logical(to, 2)) * 32 + core * 16
                        target[256 + 16 * half : 272 + 16 * half, 128 * xx : 128 * xx + 128] = held[
                            pl.ds(pl.multiple_of(start, 16), 16), pl.ds(lane, 128)
                        ]
            continue
        at = {3: 288, 4: 0, 5: 64, 6: 192}[h]
        for j in range(w // 2):
            block = core * (w // 2) + j
            x = held[pl.ds(pl.multiple_of(block * p, 32), p), :]
            live = block * SEP + iota((p, SEP), 1) < live_size(sizes, h)
            x = jnp.where(live, x, jnp.zeros_like(x))
            for target in (z0, z1) if h == 3 else (z0, z1, z2, z3):
                target[at + j * p : at + j * p + p, :] = x


def products(h, masks, left_rows, inv, u):
    me, core = position()
    p, above = PR[h], ABOVE[h]
    n = R[h] // SEP // 2
    for k, mask in enumerate(masks):
        total = None
        top = None
        for j in range(n):
            start = ((me ^ mask) & ((1 << h) - 1)) * p - (core * n + j) * SEP
            sel = one_hot(iota((p, SEP), 1) == start + iota((p, SEP), 0))
            right = inv(j)
            a = dot(sel, right, 1, 1)
            b = dot(left_rows(k, j), right, 1, 1)
            top = a if top is None else top + a
            total = b if total is None else total + b
        u[k * p : k * p + p, :] = top
        at = len(masks) * p + k * above
        u[at : at + above, :] = total


Y_ALL = (0,) + Y_MASKS
YZ_ALL = Y_ALL + tuple(16 + m for m in Y_ALL)


def product3_kernel(l0, l1, l2, l3, s, sp, u, inv):
    inv[0:128, :] = s[288:416, :]
    inv[128:256, :] = sp[288:416, :]
    lefts = (l0, l1, l2, l3)
    products(3, Y_ALL, lambda k, j: lefts[k][0:192, :], lambda j: inv[...], u)


def product4_kernel(l0, l1, l2, l3, s0, s1, s2, s3, u, inv):
    for k, s in enumerate((s0, s1, s2, s3)):
        inv[64 * k : 64 * k + 64, :] = s[0:64, :]
    lefts = (l0, l1, l2, l3)
    products(4, Y_ALL, lambda k, j: lefts[k][192:320, :], lambda j: inv[...], u)


def product5_kernel(l0, l1, l2, l3, s0, s1, s2, s3, u, inv6, inv):
    for k, s in enumerate((s0, s1, s2, s3)):
        for j in range(2):
            inv[j, 64 * k : 64 * k + 64, :] = s[64 + 64 * j : 128 + 64 * j, :]
            inv6[j, 32 * k : 32 * k + 32, :] = s[192 + 32 * j : 224 + 32 * j, :]
    lefts = (l0, l1, l2, l3)

    def left(k, j):
        at = 192 * (k // 4) + 64 * j
        return lefts[k % 4][at : at + 64, :]

    products(5, YZ_ALL, left, lambda j: inv[j], u)


def product6_kernel(l0, l1, l2, l3, mine, other, u, inv):
    for j in range(2):
        for k in range(4):
            inv[j, 64 * k : 64 * k + 32, :] = mine[j, 32 * k : 32 * k + 32, :]
            inv[j, 64 * k + 32 : 64 * k + 64, :] = other[j, 32 * k : 32 * k + 32, :]
    lefts = (l0, l1, l2, l3)

    def left(k, j):
        at = 192 * (k // 4) + 128 + 32 * j
        return lefts[k % 4][at : at + 32, :]

    products(6, YZ_ALL, left, lambda j: inv[j], u)


def finish_kernel(h, count, ua, ub, own, *ups):
    p, above = PR[h], ABOVE[h]
    cols = ua.shape[1]
    own[...] = (ua[0 : count * p, :] + ub[0 : count * p, :]).astype(BF16)
    at = 0
    for t, up in zip(range(h + 1, LEVELS + 1), ups):
        for k in range(count):
            start = count * p + k * above + at
            x = ua[start : start + PR[t], :] + ub[start : start + PR[t], :]
            hi = x.astype(BF16)
            up[k * PR[t] : (k + 1) * PR[t], 0:cols] = hi
            up[k * PR[t] : (k + 1) * PR[t], cols : 2 * cols] = (x - hi.astype(F32)).astype(BF16)
        at += PR[t]


def root_kernel(a, b, v):
    me, core = position()
    yy, xx = me & 3, lax.shift_right_logical(me, 5)
    unit = one_hot(iota((32, 32), 0) == iota((32, 32), 1))
    for k in range(4):
        for half in range(2):
            for x in range(4):
                mine = a[32 * k + 16 * half : 32 * k + 16 * half + 16, 128 * x : 128 * x + 128]
                other = b[32 * k + 16 * half : 32 * k + 16 * half + 16, 128 * x : 128 * x + 128]
                low = jnp.where(core == 0, mine.astype(F32), other.astype(F32))
                high = jnp.where(core == 0, other.astype(F32), mine.astype(F32))
                both = jnp.concatenate([low, high], 0).astype(BF16)
                flipped = dot(both, unit, 0, 0).astype(BF16)
                for y in range(4):
                    at = ((y ^ yy) * 8 + half * 4 + (x ^ xx)) * 32
                    v[pl.ds(pl.multiple_of(at, 32), 32), 32 * k : 32 * k + 32] = flipped[32 * y : 32 * y + 32, :]


def solve(leaf_rhs, leaf_inv, row_blocks, node_rhs, node_inv, sep_size):
    me = lax.axis_index("leaf")

    (s12,) = pl.pallas_call(
        first_kernel,
        out_shape=[struct((384, SEP), BF16)],
        grid=(1,),
        in_specs=[pl.BlockSpec(memory_space=pltpu.SMEM), pl.BlockSpec((1, 384, SEP), lambda i: (0, 0, 0))],
        out_specs=[pl.BlockSpec((384, SEP), lambda i: (0, 0))],
        cost_estimate=pl.CostEstimate(flops=10**6, bytes_accessed=2 * 384 * 1024, transcendentals=0),
    )(sep_size, node_inv)
    s12_1 = with_partner(s12, 1)
    s2 = s12[256:]
    inv1 = jnp.concatenate([s12[:256], s12_1[:256]], 0)
    inv2 = jnp.concatenate([s2, s12_1[256:], with_partner(s2, 2), with_partner(s2, 3)], 0)

    m0, m1, m2, mp34, mp56, z0, z1, z2, z3 = call(
        pack_kernel,
        [
            struct((448, SEP), BF16),
            struct((448, SEP), BF16),
            struct((320, SEP), BF16),
            struct((320, SEP), BF16),
            struct((192, SEP), BF16),
            struct((416, SEP), BF16),
            struct((416, SEP), BF16),
            struct((288, SEP), BF16),
            struct((288, SEP), BF16),
        ],
        (sep_size, row_blocks[0], node_inv[0]),
        [pltpu.VMEM((480, SEP), BF16)],
        smem=1,
        flops=3 * 10**9,
    )
    mp34_all = [mp34] + [with_partner(mp34, m) for m in Y_MASKS]
    z_all = [z0] + [with_partner(x, m) for x, m in zip((z1, z2, z3), Z_MASKS)]
    mp56z = with_partner(mp56, 16)

    v_own, v_up = {}, {}

    def finish(h, u, gate):
        count = 4 if h < 5 else 8
        cols = u[0].shape[1]
        shapes = [struct((count * PR[h], cols), BF16)]
        shapes += [struct((count * PR[t], 2 * cols), BF16) for t in range(h + 1, LEVELS + 1)]
        got = call(functools.partial(finish_kernel, h, count), shapes, (after(u[0], gate), u[1]), flops=10**6)
        v_own[h] = got[0]
        for t in range(h + 1, LEVELS + 1):
            v_up[t, h] = got[t - h]

    def product(h, kernel, args, gate, extra=()):
        count = 4 if h < 5 else 8
        shape = struct((count * (PR[h] + ABOVE[h]), 256), F32)
        blocks = R[h] // SEP // 2
        scratch = pltpu.VMEM((256, SEP) if blocks == 1 else (2, 256, SEP), BF16)
        got = call(kernel, [shape, *extra], (after(args[0], gate), *args[1:]), [scratch])
        return (got[0], swap_core(got[0])), got[1:]

    linv = lax.all_gather(leaf_inv, "rhs", axis=1, tiled=True)[0]
    x0 = dot(linv, leaf_rhs[0].astype(BF16))
    x0b = x0.astype(BF16)
    r1 = (node_rhs[0, :256] - dot(row_blocks[0, :256], x0b)).astype(BF16)
    g_rest = node_rhs[0, 256:] - dot(m0, x0b)

    outs = {}
    r1_all = jnp.concatenate([r1, with_partner(r1, 1)], 0)
    pair = jnp.concatenate([after(mp56, r1), mp56z], 0)
    mp56_all = [pair] + [with_partner(pair, m) for m in Y_MASKS]
    x1 = dot(inv1, r1_all, 0, 0)
    outs[1] = lax.dynamic_slice_in_dim(x1, (me & 1) * 256, 256, 0)
    g_rest = g_rest - dot(m1, x1.astype(BF16))
    r2 = g_rest[:128].astype(BF16)
    r2_all = jnp.concatenate([r2] + [with_partner(r2, m) for m in Y_MASKS], 0)
    u3, _ = product(3, product3_kernel, (*mp34_all, z_all[0], z_all[1]), r2)
    x2 = dot(inv2, r2_all, 0, 0)
    outs[2] = lax.dynamic_slice_in_dim(x2, (me & 3) * 128, 128, 0)
    g_rest = g_rest[128:] - dot(m2, x2.astype(BF16))
    g = {h: g_rest[OFF_O[h] - 384 : OFF_O[h] - 384 + PR[h]] for h in range(3, LEVELS + 1)}

    def scatter(p, masks):
        total = p[0]
        for k, m in enumerate(masks):
            total = total + with_partner(p[k + 1], m)
        return total

    up = {}
    own = {}
    for h in (3, 4, 5, 6):
        count = 1 if h < 5 else 2
        r = g[h].astype(BF16)
        if h == 3:
            r_all = [r, with_partner(r, 4)]
            finish(3, u3, r)
            u4, _ = product(4, product4_kernel, (*mp34_all, *z_all), r)
        else:
            if h == 6:
                r = jnp.concatenate([r, with_partner(r, 32)], 0)
            r_all = [r] + [with_partner(r, m) for m in Z_MASKS]
        if h == 4:
            u5, (inv6,) = product(5, product5_kernel, (*mp56_all, *z_all), r, [struct((2, 128, SEP), BF16)])
            inv6x = with_partner(inv6, 32)
        if h == 5:
            u6, _ = product(6, product6_kernel, (*mp56_all, inv6, inv6x), r)
            root_a = jnp.concatenate([x[256:288] for x in z_all], 0)
            root_b = swap_core(root_a)
            (v7,) = call(root_kernel, [struct((1024, 128), BF16)], (after(root_a, r), root_b))
        r_two = jnp.concatenate(r_all + r_all, 0)
        for t in range(h + 1, LEVELS + 1):
            term = dot(v_up[t, h], r_two).reshape(count, 4, PR[t], 128)
            term = [term[k] for k in range(count)]
            if t in up:
                term[0] = term[0] + up[t][0]
                if len(up[t]) == 2:
                    term[1] = term[1] + up[t][1]
            up[t] = term
        if h == 3:
            finish(4, u4, up[4][0])
        elif h == 4:
            finish(5, u5, up[5][0])
        elif h == 5:
            finish(6, u6, up[6][0])
        part = scatter(jnp.concatenate(up[h + 1], 1), Y_MASKS)
        if count == 1:
            g[h + 1] = g[h + 1] - part
        else:
            n = PR[h + 1]
            g[h + 1] = g[h + 1] - (part[:n] + with_partner(part[n:], 16))
        term = dot(v_own[h], jnp.concatenate(r_all, 0)).reshape(count, 4, PR[h], 128)
        own[h] = [term[k] for k in range(count)]

    r7 = g[7].astype(BF16)
    lower = [own[3][0], own[4][0], own[5][0], own[6][0], own[5][1], own[6][1]]
    lower, r7 = lax.optimization_barrier((jnp.concatenate(lower, 1), r7))
    lower = scatter(lower, Y_MASKS)
    r7_all = jnp.concatenate([r7] + [with_partner(r7, m) for m in Z_MASKS], 0)
    last = dot(v7, r7_all).reshape(4, 256, 128)
    last, lower = lax.optimization_barrier((last, lower))
    part = scatter(last, Y_MASKS).reshape(2, 4, 32, 128)
    part = scatter(part.transpose(1, 0, 2, 3).reshape(4, 64, 128), X_MASKS)
    far = with_partner(jnp.concatenate([part[32:], lower[288:]], 0), 16)
    outs[7] = part[:32] + far[:32]
    outs[3], outs[4] = lower[:128], lower[128:192]
    outs[5] = lower[192:256] + far[32:96]
    outs[6] = lower[256:288] + far[96:]
    live7 = me * 32 + iota((32, 1), 0) < sep_size[1]
    outs[7] = jnp.where(live7, outs[7], jnp.zeros_like(outs[7]))
    node_solved = jnp.concatenate([outs[h] for h in R], 0)
    return x0[None], node_solved[None]


def solution(mesh):
    in_specs = (
        P("leaf", None, "rhs"),
        P("leaf", "rhs", None),
        P("leaf", None, None),
        P("leaf", None, "rhs"),
        P("leaf", None, None),
        P(),
    )
    out_specs = (P("leaf", None, "rhs"), P("leaf", None, "rhs"))
    return jax.shard_map(solve, mesh=mesh, in_specs=in_specs, out_specs=out_specs, check_vma=False)
```

```python
import functools

import jax
import jax.numpy as jnp
from jax import lax
from jax.experimental import pallas as pl
from jax.experimental.pallas import tpu as pltpu
from jax.sharding import PartitionSpec as P


SEP = 512
LEAVES = 128
LEVELS = 7
BF16 = jnp.bfloat16
F32 = jnp.float32

Y_MASKS = (1, 2, 3)
Z_MASKS = (4, 8, 12)
X_MASKS = (32, 64, 96)
FAR = 24


def level_rows(height):
    return SEP * 2 ** ((height - 1) // 2)


R = {h: level_rows(h) for h in range(1, LEVELS + 1)}
PR = {h: R[h] >> h for h in R}
WIDTH = {h: SEP + sum(R[g] for g in range(1, h)) for h in R}
OFF_O, OFF_E, OFF_C = {}, {}, {}
_o = _e = _c = 0
for _h in R:
    OFF_O[_h], OFF_E[_h], OFF_C[_h] = _o, _e, _c
    _o += PR[_h]
    _e += PR[_h] * R[_h] // SEP
    _c += PR[_h] * WIDTH[_h] // SEP
FIRST = {1: 1}
for _h in range(2, LEVELS + 1):
    FIRST[_h] = FIRST[_h - 1] + R[_h - 1] // SEP
ABOVE = {h: sum(PR[g] for g in range(h + 1, LEVELS + 1)) for h in range(3, 7)}


def with_partner(x, mask):
    return lax.ppermute(x, "leaf", [(i, i ^ mask) for i in range(LEAVES)])


def swap_core(x):
    return lax.ppermute(x, "rhs", [(0, 1), (1, 0)])


def dot(a, b, ca=1, cb=0):
    return lax.dot_general(a, b, (((ca,), (cb,)), ((), ())), preferred_element_type=F32)


def one_hot(match):
    return jnp.where(match, 1.0, 0.0).astype(BF16)


def iota(shape, axis):
    return lax.broadcasted_iota(jnp.int32, shape, axis)


def position():
    return lax.axis_index("leaf"), lax.axis_index("rhs")


def call(kernel, out_shapes, args, scratch=(), flops=10**8, smem=0, specs=None):
    moved = sum(a.size * a.dtype.itemsize for a in args) + sum(
        s.size * s.dtype.itemsize for s in out_shapes
    )
    if specs is None:
        specs = [pl.BlockSpec(memory_space=pltpu.SMEM)] * smem
        specs += [pl.BlockSpec(memory_space=pltpu.VMEM)] * (len(args) - smem)
    return pl.pallas_call(
        kernel,
        out_shape=out_shapes,
        in_specs=specs,
        out_specs=[pl.BlockSpec(memory_space=pltpu.VMEM)] * len(out_shapes),
        scratch_shapes=list(scratch),
        compiler_params=pltpu.CompilerParams(vmem_limit_bytes=40 * 2**20),
        cost_estimate=pl.CostEstimate(flops=flops, bytes_accessed=moved, transcendentals=0),
    )(*args)


def after(x, *values):
    return lax.optimization_barrier((x, *values))[0]


def struct(shape, dtype):
    return jax.ShapeDtypeStruct(shape, dtype)


def regroup(x, rows, width):
    n = rows * width
    shift = rows.bit_length() - 1
    t = iota((n, n), 0)
    source = (t & (rows - 1)) * width + lax.shift_right_logical(t, shift)
    return dot(one_hot(source == iota((n, n), 1)), x).astype(BF16)


def live_size(sizes, h):
    return sizes[lax.shift_right_logical(LEAVES + position()[0], h)]


def first_kernel(sizes, ni, s12):
    for h, at, n in ((1, 0, 256), (2, 256, 128)):
        x = ni[0, at : at + n, :]
        live = iota((n, SEP), 1) < live_size(sizes, h)
        s12[at : at + n, :] = jnp.where(live, x, jnp.zeros_like(x))


def pack_kernel(sizes, rb, ni, m0, m1, m2, mp34, mp56, z0, z1, z2, z3, held):
    me, core = position()
    z = lax.shift_right_logical(me, 2) & 7
    for g in range(2, LEVELS + 1):
        p, w = PR[g], WIDTH[g] // SEP
        n = p * w
        held[0:n, :] = regroup(rb[OFF_C[g] : OFF_C[g] + n, :], p, w)

        def rows(j):
            return held[pl.ds(pl.multiple_of(j * p, 32), p), :]

        m0[OFF_O[g] - 256 : OFF_O[g] - 256 + p, :] = held[0:p, :]
        m1[OFF_O[g] - 256 : OFF_O[g] - 256 + p, :] = held[p : 2 * p, :]
        if g >= 3:
            m2[OFF_O[g] - 384 : OFF_O[g] - 384 + p, :] = held[2 * p : 3 * p, :]
        if g >= 4:
            at = OFF_O[g] - OFF_O[4]
            mp34[at : at + p, :] = rows(FIRST[3] + core)
        if g >= 5:
            at = 192 + OFF_O[g] - OFF_O[5]
            mp34[at : at + p, :] = rows(FIRST[4] + core)
        if g >= 6:
            at = OFF_O[g] - OFF_O[6]
            for j in range(2):
                mp56[64 * j + at : 64 * j + at + p, :] = rows(FIRST[5] + 2 * core + j)
        if g == 7:
            for j in range(2):
                mp56[128 + 32 * j : 160 + 32 * j, :] = rows(FIRST[6] + 2 * core + j)
    for h in range(3, LEVELS + 1):
        p, w = PR[h], R[h] // SEP
        n = p * w
        held[0:n, :] = regroup(ni[OFF_E[h] : OFF_E[h] + n, :], p, w)
        if h == 7:
            for k, target in enumerate((z0, z1, z2, z3)):
                for half in range(2):
                    to = z ^ k ^ (6 * half)
                    lane = pl.multiple_of((to & 3) * 128, 128)
                    for xx in range(4):
                        start = (2 * xx + lax.shift_right_logical(to, 2)) * 32 + core * 16
                        target[256 + 16 * half : 272 + 16 * half, 128 * xx : 128 * xx + 128] = held[
                            pl.ds(pl.multiple_of(start, 16), 16), pl.ds(lane, 128)
                        ]
            continue
        at = {3: 288, 4: 0, 5: 64, 6: 192}[h]
        for j in range(w // 2):
            block = core * (w // 2) + j
            x = held[pl.ds(pl.multiple_of(block * p, 32), p), :]
            live = block * SEP + iota((p, SEP), 1) < live_size(sizes, h)
            x = jnp.where(live, x, jnp.zeros_like(x))
            for target in (z0, z1) if h == 3 else (z0, z1, z2, z3):
                target[at + j * p : at + j * p + p, :] = x


def products(h, masks, left_rows, inv, u):
    me, core = position()
    p, above = PR[h], ABOVE[h]
    n = R[h] // SEP // 2
    for k, mask in enumerate(masks):
        total = None
        top = None
        for j in range(n):
            start = ((me ^ mask) & ((1 << h) - 1)) * p - (core * n + j) * SEP
            sel = one_hot(iota((p, SEP), 1) == start + iota((p, SEP), 0))
            right = inv(j)
            a = dot(sel, right, 1, 1)
            b = dot(left_rows(k, j), right, 1, 1)
            top = a if top is None else top + a
            total = b if total is None else total + b
        u[k * p : k * p + p, :] = top
        at = len(masks) * p + k * above
        u[at : at + above, :] = total


Y_ALL = (0,) + Y_MASKS
YZ_ALL = Y_ALL + tuple(FAR ^ m for m in Y_ALL)


def product3_kernel(l0, l1, l2, l3, s, sp, u, inv):
    inv[0:128, :] = s[288:416, :]
    inv[128:256, :] = sp[288:416, :]
    lefts = (l0, l1, l2, l3)
    products(3, Y_ALL, lambda k, j: lefts[k][0:192, :], lambda j: inv[...], u)


def product4_kernel(l0, l1, l2, l3, s0, s1, s2, s3, u, inv):
    for k, s in enumerate((s0, s1, s2, s3)):
        inv[64 * k : 64 * k + 64, :] = s[0:64, :]
    lefts = (l0, l1, l2, l3)
    products(4, Y_ALL, lambda k, j: lefts[k][192:320, :], lambda j: inv[...], u)


def product5_kernel(l0, l1, l2, l3, s0, s1, s2, s3, u, inv6, inv):
    for k, s in enumerate((s0, s1, s2, s3)):
        for j in range(2):
            inv[j, 64 * k : 64 * k + 64, :] = s[64 + 64 * j : 128 + 64 * j, :]
            inv6[j, 32 * k : 32 * k + 32, :] = s[192 + 32 * j : 224 + 32 * j, :]
    lefts = (l0, l1, l2, l3)

    def left(k, j):
        at = 192 * (k // 4) + 64 * j
        return lefts[k % 4][at : at + 64, :]

    products(5, YZ_ALL, left, lambda j: inv[j], u)


def product6_kernel(l0, l1, l2, l3, mine, other, u, inv):
    for j in range(2):
        for k in range(4):
            inv[j, 64 * k : 64 * k + 32, :] = mine[j, 32 * k : 32 * k + 32, :]
            inv[j, 64 * k + 32 : 64 * k + 64, :] = other[j, 32 * k : 32 * k + 32, :]
    lefts = (l0, l1, l2, l3)

    def left(k, j):
        at = 192 * (k // 4) + 128 + 32 * j
        return lefts[k % 4][at : at + 32, :]

    products(6, YZ_ALL, left, lambda j: inv[j], u)


def finish_kernel(h, count, ua, ub, own, *ups):
    p, above = PR[h], ABOVE[h]
    cols = ua.shape[1]
    own[...] = (ua[0 : count * p, :] + ub[0 : count * p, :]).astype(BF16)
    at = 0
    for t, up in zip(range(h + 1, LEVELS + 1), ups):
        for k in range(count):
            start = count * p + k * above + at
            x = ua[start : start + PR[t], :] + ub[start : start + PR[t], :]
            hi = x.astype(BF16)
            up[k * PR[t] : (k + 1) * PR[t], 0:cols] = hi
            up[k * PR[t] : (k + 1) * PR[t], cols : 2 * cols] = (x - hi.astype(F32)).astype(BF16)
        at += PR[t]


def root_kernel(a, b, v):
    me, core = position()
    yy, xx = me & 3, lax.shift_right_logical(me, 5)
    unit = one_hot(iota((32, 32), 0) == iota((32, 32), 1))
    for k in range(4):
        for half in range(2):
            for x in range(4):
                mine = a[32 * k + 16 * half : 32 * k + 16 * half + 16, 128 * x : 128 * x + 128]
                other = b[32 * k + 16 * half : 32 * k + 16 * half + 16, 128 * x : 128 * x + 128]
                low = jnp.where(core == 0, mine.astype(F32), other.astype(F32))
                high = jnp.where(core == 0, other.astype(F32), mine.astype(F32))
                both = jnp.concatenate([low, high], 0).astype(BF16)
                flipped = dot(both, unit, 0, 0).astype(BF16)
                for y in range(4):
                    at = ((y ^ yy) * 8 + half * 4 + (x ^ xx)) * 32
                    v[pl.ds(pl.multiple_of(at, 32), 32), 32 * k : 32 * k + 32] = flipped[32 * y : 32 * y + 32, :]


def solve(leaf_rhs, leaf_inv, row_blocks, node_rhs, node_inv, sep_size):
    me = lax.axis_index("leaf")

    (s12,) = pl.pallas_call(
        first_kernel,
        out_shape=[struct((384, SEP), BF16)],
        grid=(1,),
        in_specs=[pl.BlockSpec(memory_space=pltpu.SMEM), pl.BlockSpec((1, 384, SEP), lambda i: (0, 0, 0))],
        out_specs=[pl.BlockSpec((384, SEP), lambda i: (0, 0))],
        cost_estimate=pl.CostEstimate(flops=10**6, bytes_accessed=2 * 384 * 1024, transcendentals=0),
    )(sep_size, node_inv)
    s12_1 = with_partner(s12, 1)
    s2 = s12[256:]
    inv1 = jnp.concatenate([s12[:256], s12_1[:256]], 0)
    inv2 = jnp.concatenate([s2, s12_1[256:], with_partner(s2, 2), with_partner(s2, 3)], 0)

    packed = call(
        pack_kernel,
        [
            struct((448, SEP), BF16),
            struct((448, SEP), BF16),
            struct((320, SEP), BF16),
            struct((320, SEP), BF16),
            struct((192, SEP), BF16),
            struct((416, SEP), BF16),
            struct((416, SEP), BF16),
            struct((288, SEP), BF16),
            struct((288, SEP), BF16),
        ],
        (sep_size, row_blocks[0], node_inv[0]),
        [pltpu.VMEM((480, SEP), BF16)],
        smem=1,
        flops=3 * 10**9,
    )
    m0, m1, m2, mp34, mp56, z0, z1, z2, z3 = packed
    mp34_all = [mp34] + [with_partner(mp34, m) for m in Y_MASKS]
    z_all = [z0] + [with_partner(x, m) for x, m in zip((z1, z2, z3), Z_MASKS)]
    mp56z = with_partner(mp56, FAR)

    v_own, v_up = {}, {}

    def finish(h, u, gate):
        count = 4 if h < 5 else 8
        cols = u[0].shape[1]
        shapes = [struct((count * PR[h], cols), BF16)]
        shapes += [struct((count * PR[t], 2 * cols), BF16) for t in range(h + 1, LEVELS + 1)]
        got = call(functools.partial(finish_kernel, h, count), shapes, (after(u[0], gate), u[1]), flops=10**6)
        v_own[h] = got[0]
        for t in range(h + 1, LEVELS + 1):
            v_up[t, h] = got[t - h]

    def product(h, kernel, args, gate, extra=()):
        count = 4 if h < 5 else 8
        shape = struct((count * (PR[h] + ABOVE[h]), 256), F32)
        blocks = R[h] // SEP // 2
        scratch = pltpu.VMEM((256, SEP) if blocks == 1 else (2, 256, SEP), BF16)
        got = call(kernel, [shape, *extra], (after(args[0], gate), *args[1:]), [scratch])
        return (got[0], swap_core(got[0])), got[1:]

    rhs = leaf_rhs[0].astype(BF16)
    here, there = dot(leaf_inv[0], rhs), dot(swap_core(leaf_inv[0]), rhs)
    first_core = lax.axis_index("rhs") == 0
    x0 = jnp.concatenate([jnp.where(first_core, here, there), jnp.where(first_core, there, here)], 0)
    x0b = x0.astype(BF16)
    r1 = (node_rhs[0, :256] - dot(row_blocks[0, :256], x0b)).astype(BF16)
    g_rest = node_rhs[0, 256:] - dot(m0, x0b)

    outs = {}
    r1_all = jnp.concatenate([r1, with_partner(r1, 1)], 0)
    pair = jnp.concatenate([after(mp56, r1), mp56z], 0)
    mp56_all = [pair] + [with_partner(pair, m) for m in Y_MASKS]
    x1 = dot(inv1, r1_all, 0, 0)
    outs[1] = lax.dynamic_slice_in_dim(x1, (me & 1) * 256, 256, 0)
    g_rest = g_rest - dot(m1, x1.astype(BF16))
    r2 = g_rest[:128].astype(BF16)
    r2_all = jnp.concatenate([r2] + [with_partner(r2, m) for m in Y_MASKS], 0)
    u3, _ = product(3, product3_kernel, (*mp34_all, z_all[0], z_all[1]), r2)
    x2 = dot(inv2, r2_all, 0, 0)
    outs[2] = lax.dynamic_slice_in_dim(x2, (me & 3) * 128, 128, 0)
    g_rest = g_rest[128:] - dot(m2, x2.astype(BF16))
    g = {h: g_rest[OFF_O[h] - 384 : OFF_O[h] - 384 + PR[h]] for h in range(3, LEVELS + 1)}

    def scatter(p, masks):
        total = p[0]
        for k, m in enumerate(masks):
            total = total + with_partner(p[k + 1], m)
        return total

    up = {}
    own = {}
    for h in (3, 4, 5, 6):
        count = 1 if h < 5 else 2
        r = g[h].astype(BF16)
        if h == 3:
            r_all = [r, with_partner(r, 4)]
            finish(3, u3, r)
            u4, _ = product(4, product4_kernel, (*mp34_all, *z_all), r)
        else:
            if h == 6:
                r = jnp.concatenate([r, with_partner(r, 32)], 0)
            r_all = [r] + [with_partner(r, m) for m in Z_MASKS]
        if h == 4:
            u5, (inv6,) = product(5, product5_kernel, (*mp56_all, *z_all), r, [struct((2, 128, SEP), BF16)])
            inv6x = with_partner(inv6, 32)
        if h == 5:
            u6, _ = product(6, product6_kernel, (*mp56_all, inv6, inv6x), r)
            root_a = jnp.concatenate([x[256:288] for x in z_all], 0)
            root_b = swap_core(root_a)
            (v7,) = call(root_kernel, [struct((1024, 128), BF16)], (after(root_a, r), root_b))
        r_two = jnp.concatenate(r_all + r_all, 0)
        for t in range(h + 1, LEVELS + 1):
            term = dot(v_up[t, h], r_two).reshape(count, 4, PR[t], 128)
            term = [term[k] for k in range(count)]
            if t in up:
                term[0] = term[0] + up[t][0]
                if len(up[t]) == 2:
                    term[1] = term[1] + up[t][1]
            up[t] = term
        if h == 3:
            finish(4, u4, up[4][0])
        elif h == 4:
            finish(5, u5, up[5][0])
        elif h == 5:
            finish(6, u6, up[6][0])
        part = scatter(jnp.concatenate(up[h + 1], 1), Y_MASKS)
        if count == 1:
            g[h + 1] = g[h + 1] - part
        else:
            n = PR[h + 1]
            g[h + 1] = g[h + 1] - (part[:n] + with_partner(part[n:], FAR))
        term = dot(v_own[h], jnp.concatenate(r_all, 0)).reshape(count, 4, PR[h], 128)
        own[h] = [term[k] for k in range(count)]

    r7 = g[7].astype(BF16)
    lower = [own[3][0], own[4][0], own[5][0], own[6][0], own[5][1], own[6][1]]
    lower, r7 = lax.optimization_barrier((jnp.concatenate(lower, 1), r7))
    lower = scatter(lower, Y_MASKS)
    r7_all = jnp.concatenate([r7] + [with_partner(r7, m) for m in Z_MASKS], 0)
    last = dot(v7, r7_all).reshape(4, 256, 128)
    last, lower = lax.optimization_barrier((last, lower))
    part = scatter(last, Y_MASKS).reshape(2, 4, 32, 128)
    part = scatter(part.transpose(1, 0, 2, 3).reshape(4, 64, 128), X_MASKS)
    far = with_partner(jnp.concatenate([part[32:], lower[288:]], 0), FAR)
    outs[7] = part[:32] + far[:32]
    outs[3], outs[4] = lower[:128], lower[128:192]
    outs[5] = lower[192:256] + far[32:96]
    outs[6] = lower[256:288] + far[96:]
    live7 = me * 32 + iota((32, 1), 0) < sep_size[1]
    outs[7] = jnp.where(live7, outs[7], jnp.zeros_like(outs[7]))
    node_solved = jnp.concatenate([outs[h] for h in R], 0)
    return x0[None], node_solved[None]


def solution(mesh):
    in_specs = (
        P("leaf", None, "rhs"),
        P("leaf", "rhs", None),
        P("leaf", None, None),
        P("leaf", None, "rhs"),
        P("leaf", None, None),
        P(),
    )
    out_specs = (P("leaf", None, "rhs"), P("leaf", None, "rhs"))
    return jax.shard_map(solve, mesh=mesh, in_specs=in_specs, out_specs=out_specs, check_vma=False)
```

```python
import functools

import jax
import jax.numpy as jnp
from jax import lax
from jax.experimental import pallas as pl
from jax.experimental.pallas import tpu as pltpu
from jax.sharding import PartitionSpec as P


SEP = 512
LEAVES = 128
LEVELS = 7
BF16 = jnp.bfloat16
F32 = jnp.float32

Y_MASKS = (1, 2, 3)
Z_MASKS = (4, 8, 12)
X_MASKS = (32, 64, 96)
FAR = 24


def level_rows(height):
    return SEP * 2 ** ((height - 1) // 2)


R = {h: level_rows(h) for h in range(1, LEVELS + 1)}
PR = {h: R[h] >> h for h in R}
WIDTH = {h: SEP + sum(R[g] for g in range(1, h)) for h in R}
OFF_O, OFF_E, OFF_C = {}, {}, {}
_o = _e = _c = 0
for _h in R:
    OFF_O[_h], OFF_E[_h], OFF_C[_h] = _o, _e, _c
    _o += PR[_h]
    _e += PR[_h] * R[_h] // SEP
    _c += PR[_h] * WIDTH[_h] // SEP
FIRST = {1: 1}
for _h in range(2, LEVELS + 1):
    FIRST[_h] = FIRST[_h - 1] + R[_h - 1] // SEP
ABOVE = {h: sum(PR[g] for g in range(h + 1, LEVELS + 1)) for h in range(3, 7)}


def with_partner(x, mask):
    return lax.ppermute(x, "leaf", [(i, i ^ mask) for i in range(LEAVES)])


def swap_core(x):
    return lax.ppermute(x, "rhs", [(0, 1), (1, 0)])


def dot(a, b, ca=1, cb=0):
    return lax.dot_general(a, b, (((ca,), (cb,)), ((), ())), preferred_element_type=F32)


def one_hot(match):
    return jnp.where(match, 1.0, 0.0).astype(BF16)


def iota(shape, axis):
    return lax.broadcasted_iota(jnp.int32, shape, axis)


def position():
    return lax.axis_index("leaf"), lax.axis_index("rhs")


def call(kernel, out_shapes, args, scratch=(), flops=10**8, smem=0, specs=None):
    moved = sum(a.size * a.dtype.itemsize for a in args) + sum(
        s.size * s.dtype.itemsize for s in out_shapes
    )
    if specs is None:
        specs = [pl.BlockSpec(memory_space=pltpu.SMEM)] * smem
        specs += [pl.BlockSpec(memory_space=pltpu.VMEM)] * (len(args) - smem)
    return pl.pallas_call(
        kernel,
        out_shape=out_shapes,
        in_specs=specs,
        out_specs=[pl.BlockSpec(memory_space=pltpu.VMEM)] * len(out_shapes),
        scratch_shapes=list(scratch),
        compiler_params=pltpu.CompilerParams(vmem_limit_bytes=40 * 2**20),
        cost_estimate=pl.CostEstimate(flops=flops, bytes_accessed=moved, transcendentals=0),
    )(*args)


def after(x, *values):
    return lax.optimization_barrier((x, *values))[0]


def struct(shape, dtype):
    return jax.ShapeDtypeStruct(shape, dtype)


def regroup(x, rows, width):
    n = rows * width
    shift = rows.bit_length() - 1
    t = iota((n, n), 0)
    source = (t & (rows - 1)) * width + lax.shift_right_logical(t, shift)
    return dot(one_hot(source == iota((n, n), 1)), x).astype(BF16)


def live_size(sizes, h):
    return sizes[lax.shift_right_logical(LEAVES + position()[0], h)]


def first_kernel(sizes, ni, s12, s1, s2):
    for h, at, n, alone in ((1, 0, 256, s1), (2, 256, 128, s2)):
        x = ni[0, at : at + n, :]
        live = iota((n, SEP), 1) < live_size(sizes, h)
        x = jnp.where(live, x, jnp.zeros_like(x))
        s12[at : at + n, :] = x
        alone[...] = x


def level1_kernel(s1, s12_1, r, rp, m1, g, out, r2, rest):
    x = dot(s1[...], r[...], 0, 0) + dot(s12_1[0:256, :], rp[...], 0, 0)
    s1_rows = (position()[0] & 1) == 0
    out[...] = jnp.where(s1_rows, x[0:256, :], x[256:512, :])
    g2 = g[...] - dot(m1[...], x.astype(BF16))
    r2[...] = g2[0:128, :].astype(BF16)
    rest[...] = g2[128:448, :]


def level2_kernel(s2, s12_1, s2_2, s2_3, ra, rb, rc, rd, m2, g, out, r3, g4, g5, g6, g7):
    x = dot(s2[...], ra[...], 0, 0) + dot(s12_1[256:384, :], rb[...], 0, 0)
    x = x + dot(s2_2[...], rc[...], 0, 0) + dot(s2_3[...], rd[...], 0, 0)
    place = position()[0] & 3
    low = jnp.where((place & 1) == 0, x[0:128, :], x[128:256, :])
    high = jnp.where((place & 1) == 0, x[256:384, :], x[384:512, :])
    out[...] = jnp.where((place & 2) == 0, low, high)
    rest = g[...] - dot(m2[...], x.astype(BF16))
    r3[...] = rest[0:128, :].astype(BF16)
    at = 128
    for target in (g4, g5, g6, g7):
        target[...] = rest[at : at + target.shape[0], :]
        at += target.shape[0]


def pack_kernel(sizes, rb, ni, m0, m1, m2, mp34, mp5, wide, z0, z1, z2, z3, held):
    me, core = position()
    z = lax.shift_right_logical(me, 2) & 7
    for g in range(2, LEVELS + 1):
        p, w = PR[g], WIDTH[g] // SEP
        n = p * w
        held[0:n, :] = regroup(rb[OFF_C[g] : OFF_C[g] + n, :], p, w)

        def rows(j):
            return held[pl.ds(pl.multiple_of(j * p, 32), p), :]

        m0[OFF_O[g] - 256 : OFF_O[g] - 256 + p, :] = held[0:p, :]
        m1[OFF_O[g] - 256 : OFF_O[g] - 256 + p, :] = held[p : 2 * p, :]
        if g >= 3:
            m2[OFF_O[g] - 384 : OFF_O[g] - 384 + p, :] = held[2 * p : 3 * p, :]
        if g >= 4:
            at = OFF_O[g] - OFF_O[4]
            mp34[at : at + p, :] = rows(FIRST[3] + core)
        if g >= 5:
            at = 192 + OFF_O[g] - OFF_O[5]
            mp34[at : at + p, :] = rows(FIRST[4] + core)
        if g >= 6:
            at = OFF_O[g] - OFF_O[6]
            for j in range(2):
                x = rows(FIRST[5] + 2 * core + j)
                mp5[64 * j + at : 64 * j + at + p, :] = x
                wide[64 * j + at : 64 * j + at + p, :] = x
        if g == 7:
            for j in range(2):
                wide[128 + 32 * j : 160 + 32 * j, :] = rows(FIRST[6] + 2 * core + j)
        if g == 7:
            wide[192:320, :] = jnp.zeros((128, SEP), BF16)
    for h in range(3, LEVELS + 1):
        p, w = PR[h], R[h] // SEP
        n = p * w
        held[0:n, :] = regroup(ni[OFF_E[h] : OFF_E[h] + n, :], p, w)
        if h == 7:
            for k, target in enumerate((z0, z1, z2, z3)):
                for half in range(2):
                    to = z ^ k ^ (6 * half)
                    lane = pl.multiple_of((to & 3) * 128, 128)
                    for xx in range(4):
                        start = (2 * xx + lax.shift_right_logical(to, 2)) * 32 + core * 16
                        target[256 + 16 * half : 272 + 16 * half, 128 * xx : 128 * xx + 128] = held[
                            pl.ds(pl.multiple_of(start, 16), 16), pl.ds(lane, 128)
                        ]
            continue
        at = {3: 288, 4: 0, 5: 64, 6: 192}[h]
        for j in range(w // 2):
            block = core * (w // 2) + j
            x = held[pl.ds(pl.multiple_of(block * p, 32), p), :]
            live = block * SEP + iota((p, SEP), 1) < live_size(sizes, h)
            x = jnp.where(live, x, jnp.zeros_like(x))
            for target in (z0, z1) if h == 3 else (z0, z1, z2, z3):
                target[at + j * p : at + j * p + p, :] = x


def products(h, masks, left_rows, inv, u):
    me, core = position()
    p, above = PR[h], ABOVE[h]
    n = R[h] // SEP // 2
    for k, mask in enumerate(masks):
        total = None
        top = None
        for j in range(n):
            start = ((me ^ mask) & ((1 << h) - 1)) * p - (core * n + j) * SEP
            sel = one_hot(iota((p, SEP), 1) == start + iota((p, SEP), 0))
            right = inv(j)
            a = dot(sel, right, 1, 1)
            b = dot(left_rows(k, j), right, 1, 1)
            top = a if top is None else top + a
            total = b if total is None else total + b
        u[k * p : k * p + p, :] = top
        at = len(masks) * p + k * above
        u[at : at + above, :] = total


Y_ALL = (0,) + Y_MASKS
YZ_ALL = Y_ALL + tuple(FAR ^ m for m in Y_ALL)


def product3_kernel(l0, l1, l2, l3, s, sp, u, inv):
    inv[0:128, :] = s[288:416, :]
    inv[128:256, :] = sp[288:416, :]
    lefts = (l0, l1, l2, l3)
    products(3, Y_ALL, lambda k, j: lefts[k][0:192, :], lambda j: inv[...], u)


def product4_kernel(l0, l1, l2, l3, s0, s1, s2, s3, u, inv):
    for k, s in enumerate((s0, s1, s2, s3)):
        inv[64 * k : 64 * k + 64, :] = s[0:64, :]
    lefts = (l0, l1, l2, l3)
    products(4, Y_ALL, lambda k, j: lefts[k][192:320, :], lambda j: inv[...], u)


def product5_kernel(l0, l1, l2, l3, s0, s1, s2, s3, u, inv6, inv):
    for k, s in enumerate((s0, s1, s2, s3)):
        for j in range(2):
            inv[j, 64 * k : 64 * k + 64, :] = s[64 + 64 * j : 128 + 64 * j, :]
            inv6[j, 32 * k : 32 * k + 32, :] = s[192 + 32 * j : 224 + 32 * j, :]
    lefts = (l0, l1, l2, l3)

    def left(k, j):
        at = 192 * (k // 4) + 64 * j
        return lefts[k % 4][at : at + 64, :]

    products(5, YZ_ALL, left, lambda j: inv[j], u)


def product6_kernel(l0, l1, l2, l3, i0, i1, i2, i3, u, inv):
    for j in range(2):
        for k in range(4):
            for n, piece in enumerate((i0, i1, i2, i3)):
                at = 128 * k + 32 * n
                inv[j, at : at + 32, :] = piece[j, 32 * k : 32 * k + 32, :]
    lefts = (l0, l1, l2, l3)
    products(6, Y_ALL, lambda k, j: lefts[k][128 + 32 * j : 160 + 32 * j, :], lambda j: inv[j], u)


def finish_kernel(h, count, ua, ub, own, *ups):
    p, above = PR[h], ABOVE[h]
    cols = ua.shape[1]
    own[...] = (ua[0 : count * p, :] + ub[0 : count * p, :]).astype(BF16)
    at = 0
    for t, up in zip(range(h + 1, LEVELS + 1), ups):
        for k in range(count):
            start = count * p + k * above + at
            x = ua[start : start + PR[t], :] + ub[start : start + PR[t], :]
            hi = x.astype(BF16)
            up[k * PR[t] : (k + 1) * PR[t], 0:cols] = hi
            up[k * PR[t] : (k + 1) * PR[t], cols : 2 * cols] = (x - hi.astype(F32)).astype(BF16)
        at += PR[t]


def root_kernel(sizes, a, b, v):
    me, core = position()
    yy, xx = me & 3, lax.shift_right_logical(me, 5)
    unit = one_hot(iota((32, 32), 0) == iota((32, 32), 1))
    for k in range(4):
        for half in range(2):
            for x in range(4):
                mine = a[32 * k + 16 * half : 32 * k + 16 * half + 16, 128 * x : 128 * x + 128]
                other = b[32 * k + 16 * half : 32 * k + 16 * half + 16, 128 * x : 128 * x + 128]
                low = jnp.where(core == 0, mine.astype(F32), other.astype(F32))
                high = jnp.where(core == 0, other.astype(F32), mine.astype(F32))
                both = jnp.concatenate([low, high], 0).astype(BF16)
                flipped = dot(both, unit, 0, 0).astype(BF16)
                z = (lax.shift_right_logical(me, 2) & 7) ^ (6 * half)
                row = x * 1024 + z * 128 + iota((128, 32), 0)
                flipped = jnp.where(row < sizes[1], flipped, jnp.zeros_like(flipped))
                for y in range(4):
                    at = ((y ^ yy) * 8 + half * 4 + (x ^ xx)) * 32
                    v[pl.ds(pl.multiple_of(at, 32), 32), 32 * k : 32 * k + 32] = flipped[32 * y : 32 * y + 32, :]


def solve(leaf_rhs, leaf_inv, row_blocks, node_rhs, node_inv, sep_size):
    s12, s1, s2 = pl.pallas_call(
        first_kernel,
        out_shape=[struct((384, SEP), BF16), struct((256, SEP), BF16), struct((128, SEP), BF16)],
        grid=(1,),
        in_specs=[pl.BlockSpec(memory_space=pltpu.SMEM), pl.BlockSpec((1, 384, SEP), lambda i: (0, 0, 0))],
        out_specs=[pl.BlockSpec((n, SEP), lambda i: (0, 0)) for n in (384, 256, 128)],
        cost_estimate=pl.CostEstimate(flops=10**6, bytes_accessed=2 * 384 * 1024, transcendentals=0),
    )(sep_size, node_inv)
    s12_1 = with_partner(s12, 1)
    s2_2, s2_3 = with_partner(s2, 2), with_partner(s2, 3)

    packed = call(
        pack_kernel,
        [
            struct((448, SEP), BF16),
            struct((448, SEP), BF16),
            struct((320, SEP), BF16),
            struct((320, SEP), BF16),
            struct((128, SEP), BF16),
            struct((320, SEP), BF16),
            struct((416, SEP), BF16),
            struct((416, SEP), BF16),
            struct((288, SEP), BF16),
            struct((288, SEP), BF16),
        ],
        (sep_size, row_blocks[0], node_inv[0]),
        [pltpu.VMEM((480, SEP), BF16)],
        smem=1,
        flops=3 * 10**9,
    )
    m0, m1, m2, mp34, mp5, wide, z0, z1, z2, z3 = packed
    mp34_all = [mp34] + [with_partner(mp34, m) for m in Y_MASKS]
    z_all = [z0] + [with_partner(x, m) for x, m in zip((z1, z2, z3), Z_MASKS)]
    mp5_far = with_partner(mp5, FAR)

    v_own, v_up = {}, {}

    def finish(h, u, gate):
        count = 8 if h == 5 else 4
        cols = u[0].shape[1]
        shapes = [struct((count * PR[h], cols), BF16)]
        shapes += [struct((count * PR[t], 2 * cols), BF16) for t in range(h + 1, LEVELS + 1)]
        got = call(functools.partial(finish_kernel, h, count), shapes, (after(u[0], gate), u[1]), flops=10**6)
        v_own[h] = got[0]
        for t in range(h + 1, LEVELS + 1):
            v_up[t, h] = got[t - h]

    def product(h, kernel, args, gate, extra=()):
        count = 8 if h == 5 else 4
        cols = 512 if h == 6 else 256
        shape = struct((count * (PR[h] + ABOVE[h]), cols), F32)
        blocks = R[h] // SEP // 2
        scratch = pltpu.VMEM((256, SEP) if blocks == 1 else (2, cols, SEP), BF16)
        got = call(kernel, [shape, *extra], (after(args[0], gate), *args[1:]), [scratch])
        return (got[0], swap_core(got[0])), got[1:]

    rhs = leaf_rhs[0].astype(BF16)
    here, there = dot(leaf_inv[0], rhs), dot(swap_core(leaf_inv[0]), rhs)
    first_core = lax.axis_index("rhs") == 0
    x0 = jnp.concatenate([jnp.where(first_core, here, there), jnp.where(first_core, there, here)], 0)
    x0b = x0.astype(BF16)
    r1 = (node_rhs[0, :256] - dot(row_blocks[0, :256], x0b)).astype(BF16)
    g_rest = node_rhs[0, 256:] - dot(m0, x0b)

    outs = {}
    r1_other = with_partner(r1, 1)
    outs[1], r2, g_rest = call(
        level1_kernel,
        [struct((256, 128), F32), struct((128, 128), BF16), struct((320, 128), F32)],
        (s1, s12_1, r1, r1_other, m1, g_rest),
    )
    r2_all = [r2] + [with_partner(r2, m) for m in Y_MASKS]
    u3, _ = product(3, product3_kernel, (*mp34_all, z_all[0], z_all[1]), r2)
    outs[2], r3, *g_list = call(
        level2_kernel,
        [struct((128, 128), F32), struct((128, 128), BF16)] + [struct((PR[h], 128), F32) for h in (4, 5, 6, 7)],
        (s2, s12_1, s2_2, s2_3, *r2_all, m2, g_rest),
    )
    g = dict(zip((4, 5, 6, 7), g_list))
    wide = lax.dynamic_update_slice(after(wide, r3), mp5_far, (192, 0))
    mp56_all = [wide] + [with_partner(wide, m) for m in Y_MASKS]

    def scatter(p, masks):
        total = p[0]
        for k, m in enumerate(masks):
            total = total + with_partner(p[k + 1].astype(BF16), m).astype(F32)
        return total

    up = {}
    own = {}
    for h in (3, 4, 5, 6):
        count = 2 if h == 5 else 1
        if h == 3:
            r = r3
        elif h < 6:
            r = g[h].astype(BF16)
        if h == 3:
            r_all = [r, with_partner(r, 4)]
            finish(3, u3, r)
            u4, _ = product(4, product4_kernel, (*mp34_all, *z_all), r)
        else:
            if h == 6:
                r = jnp.concatenate([g[6].astype(BF16), g6_far.astype(BF16)], 0)
                r = jnp.concatenate([r, with_partner(r, 32)], 0)
            r_all = [r] + [with_partner(r, m) for m in Z_MASKS]
        if h == 4:
            u5, (inv6,) = product(5, product5_kernel, (*mp56_all, *z_all), r, [struct((2, 128, SEP), BF16)])
            inv6_all = [inv6] + [with_partner(inv6, m) for m in (FAR, 32, FAR ^ 32)]
        if h == 5:
            u6, _ = product(6, product6_kernel, (*mp56_all, *inv6_all), r)
            root_a = jnp.concatenate([x[256:288] for x in z_all], 0)
            root_b = swap_core(root_a)
            (v7,) = call(
                root_kernel, [struct((1024, 128), BF16)], (sep_size, after(root_a, r), root_b), smem=1
            )
        r_two = jnp.concatenate(r_all + r_all, 0)
        for t in range(h + 1, LEVELS + 1):
            term = dot(v_up[t, h], r_two).reshape(count, 4, PR[t], 128)
            term = [term[k] for k in range(count)]
            if t in up:
                term[0] = term[0] + up[t][0]
            up[t] = term
        if h == 3:
            finish(4, u4, up[4][0])
        elif h == 4:
            finish(5, u5, up[5][0])
        elif h == 5:
            finish(6, u6, up[6][0])
        if h == 5:
            part = scatter(jnp.concatenate([up[6][0], up[6][1], up[7][1]], 1), Y_MASKS)
            near = g[6] - part[:32]
            got = with_partner(jnp.concatenate([near, part[32:]], 0), FAR)
            g[6] = near - got[32:64]
            g6_far = got[:32] - part[32:64]
            g[7] = g[7] - got[64:]
        else:
            g[h + 1] = g[h + 1] - scatter(up[h + 1][0], Y_MASKS)
        term = dot(v_own[h], jnp.concatenate(r_all, 0)).reshape(count, 4, PR[h], 128)
        own[h] = [term[k] for k in range(count)]

    r7 = g[7].astype(BF16)
    lower = [own[3][0], own[4][0], own[5][0], own[6][0], own[5][1]]
    lower, r7 = lax.optimization_barrier((jnp.concatenate(lower, 1), r7))
    lower = scatter(lower, Y_MASKS)
    r7_all = jnp.concatenate([r7] + [with_partner(r7, m) for m in Z_MASKS], 0)
    last = dot(v7, r7_all).reshape(4, 256, 128)
    part = scatter(last, Y_MASKS).reshape(2, 4, 32, 128)
    part = scatter(part.transpose(1, 0, 2, 3).reshape(4, 64, 128), X_MASKS)
    far = with_partner(jnp.concatenate([part[32:], lower[288:]], 0).astype(BF16), FAR).astype(F32)
    outs[7] = part[:32] + far[:32]
    outs[3], outs[4] = lower[:128], lower[128:192]
    outs[5] = lower[192:256] + far[32:96]
    outs[6] = lower[256:288]
    node_solved = jnp.concatenate([outs[h] for h in R], 0)
    return x0[None], node_solved[None]


def solution(mesh):
    in_specs = (
        P("leaf", None, "rhs"),
        P("leaf", "rhs", None),
        P("leaf", None, None),
        P("leaf", None, "rhs"),
        P("leaf", None, None),
        P(),
    )
    out_specs = (P("leaf", None, "rhs"), P("leaf", None, "rhs"))
    return jax.shard_map(solve, mesh=mesh, in_specs=in_specs, out_specs=out_specs, check_vma=False)
```
